256 devices in a mesh: src: 32 (over z_hi, x, core), tgt: 8 (over y, z_lo).
Axes of the slice: x: 4, y: 4, z: 8 (z_hi: 4, z_lo: 2; z = z_hi * 2 + z_lo), core: 2. Of those that a mesh axis runs over, the one named last changes fastest.
Arguments:
- upstream: bfloat16 [256, 128, 324], P('src'), may hold values from -6 to 6
- centers: int32 [2, 256, 128], P(None, 'src'), may hold values from -4 to 259, as said below
- post_relu: bfloat16 [256, 128, 128], P('src'), as said below
- conv_input: bfloat16 [256, 128, 128], P(('src', 'tgt')), may hold values from -6 to 6
- target_feats: bfloat16 [64, 256, 256], P('tgt'), may hold values from -6 to 6
- out_weight: bfloat16 [128, 256], replicated, may hold values from -0.5 to 0.5
- conv_weight: bfloat16 [3, 3, 128, 128], replicated, may hold values from -0.1875 to 0.1875
Outputs:
- tgt_grad: bfloat16 [64, 256, 256], P('tgt', 'src')
- act_grad: bfloat16 [256, 128, 128], P(('src', 'tgt'))
- out_wgrad: float32 [128, 256], replicated
- conv_wgrad: float32 [3, 3, 128, 128], replicated
The draws below stay inside these ranges and needn't reach their ends.
Inputs may be any that keep to these rules, and one draw needn't show every extreme that they name: centers[0] is a target row from -4 to 67 and centers[1] a target column from -4 to 259; windows may reach outside the target image. `post_relu`: entries are zero or positive.
All inputs are finite; a program needn't handle non-finite values.
Results may differ from the reference program's by a relative error of at most 0.0064.
Values may be sent and summed in bfloat16 or wider, within the bound.
No kernel may reach another device: no remote copies, remote signals or barrier semaphores. Data moves between devices by JAX's collectives and lax.ppermute only.
A program may use at most 64 MiB of HBM per device.

```python
import math
import jax
import jax.numpy as jnp
from jax import lax

D = 256
CH = 128
WIN = 324
SW = 128
TW = 256
SH = 256
TH = 64


def draw_centers(key, part):
    row_key = jax.random.fold_in(key, 11)
    col_key = jax.random.fold_in(key, 12)
    row_vals = jax.random.randint(row_key, (1, SH, SW), -4, TH + 4, dtype=jnp.int32)
    col_vals = jax.random.randint(col_key, (1, SH, SW), -4, TW + 4, dtype=jnp.int32)
    return jnp.concatenate([row_vals, col_vals], axis=0)


def draw_post_relu(key, part):
    values = jax.random.normal(key, (SH, SW, CH), jnp.float32)
    return jnp.maximum(values, 0.0).astype(jnp.bfloat16)


def shard_levels(stream_key, shape, cuts, low, top_value):
    def one(position, shards_of):
        steps = jax.random.uniform(jax.random.fold_in(jax.random.fold_in(stream_key, 6), position), (shards_of,), jnp.float32, low / len(cuts), top_value / len(cuts))
        return jnp.repeat(jnp.exp(steps), shape[position] // shards_of).reshape((-1,) + (1,) * (len(shape) - position - 1))

    gain = one(*cuts[0])
    for cut in cuts[1:]:
        gain = gain * one(*cut)
    return gain


def centred(key, dims, spread, reach, cuts=(), kind=jnp.bfloat16):
    array = jax.random.normal(key, dims, jnp.float32) * spread
    if len(cuts) > 0:
        array = shard_levels(key, dims, cuts, -0.22, 0.18) * array
    return jnp.clip(array, min=-reach, max=reach).astype(kind)


def setup_inputs(seed: int = 0) -> dict:
    splits = jax.random.split(jax.random.key(seed), 8)
    return {
        "upstream": centred(splits[0], (SH, SW, WIN), 1.0, 6.0, ((0, 32),)),
        "centers": draw_centers(jax.random.fold_in(splits[7], 71), 0),
        "post_relu": draw_post_relu(jax.random.fold_in(splits[7], 71), 0),
        "conv_input": centred(splits[3], (SH, SW, CH), 1.0, 6.0, ((0, 256),)),
        "target_feats": centred(splits[4], (TH, TW, D), 1.0, 6.0, ((0, 8),)),
        "out_weight": centred(splits[5], (CH, D), CH ** -0.5, 0.5),
        "conv_weight": centred(splits[6], (3, 3, CH, CH), (9 * CH) ** -0.5, 0.1875),
    }


def settle(value):
    return lax.optimization_barrier(value).astype(jnp.float32)

def corr_block(center_rows, center_cols, grad_rows, row_start, row_total, col_total):
    source_total = grad_rows.shape[0]
    row_ids = row_start + jnp.arange(row_total, dtype=jnp.int32)
    col_ids = jnp.arange(col_total, dtype=jnp.int32)
    offsets = jnp.arange(9, dtype=jnp.int32)
    row_parts = []
    col_parts = []
    for level_no in range(4):
        level_step = 2 ** level_no
        row_off = jnp.floor_divide(row_ids, level_step)[None, :] - jnp.floor_divide(center_rows, level_step)[:, None] + 4
        col_off = jnp.floor_divide(col_ids, level_step)[None, :] - jnp.floor_divide(center_cols, level_step)[:, None] + 4
        row_hot = jnp.where(row_off[:, None, :] == offsets[None, :, None], 0.25 ** level_no, 0.0).astype(jnp.float32)
        col_hot = jnp.where(col_off[:, None, :] == offsets[None, :, None], 1.0, 0.0).astype(jnp.float32)
        level_grads = grad_rows[:, 81 * level_no:81 * (level_no + 1)].astype(jnp.float32).reshape(source_total, 9, 9)
        row_parts.append(row_hot)
        col_parts.append(jnp.einsum('sab,sbx->sax', level_grads, col_hot))
    row_table = jnp.concatenate(row_parts, axis=1)
    col_table = jnp.concatenate(col_parts, axis=1)
    return jnp.einsum('say,sax->syx', row_table, col_table).astype(jnp.bfloat16)

def reference(upstream, centers, post_relu, conv_input, target_feats, out_weight, conv_weight):
    source_total = SH * SW
    flat_grads = upstream.reshape(source_total, WIN)
    flat_rows = centers[0].reshape(source_total)
    flat_cols = centers[1].reshape(source_total)
    relu_flat = post_relu.reshape(source_total, CH).astype(jnp.float32)
    src_feats = jnp.dot(relu_flat, out_weight.astype(jnp.float32), preferred_element_type=jnp.float32).astype(jnp.bfloat16)
    feats_f = settle(src_feats)
    flat_targets = target_feats.reshape(TH * TW, D).astype(jnp.float32)
    block_size = 4 * SW
    inv_root = 1.0 / math.sqrt(D)

    def accumulate(target_acc, block_no):
        first_row = block_no * block_size
        corr_rows = corr_block(lax.dynamic_slice_in_dim(flat_rows, first_row, block_size), lax.dynamic_slice_in_dim(flat_cols, first_row, block_size), lax.dynamic_slice_in_dim(flat_grads, first_row, block_size, 0), jnp.int32(0), TH, TW)
        corr_rows = settle(corr_rows.reshape(block_size, TH * TW))
        feat_rows = lax.dynamic_slice_in_dim(feats_f, first_row, block_size, 0)
        src_part = jnp.dot(corr_rows, flat_targets, preferred_element_type=jnp.float32) * inv_root
        return (target_acc + jnp.dot(corr_rows.T, feat_rows, preferred_element_type=jnp.float32), src_part)
    target_acc, src_parts = lax.scan(accumulate, jnp.zeros((TH * TW, D), jnp.float32), jnp.arange(SH // 4, dtype=jnp.int32))
    tgt_grad = (target_acc * inv_root).reshape(TH, TW, D).astype(jnp.bfloat16)
    src_grad = src_parts.reshape(SH, SW, D).astype(jnp.bfloat16)
    grad_f = settle(src_grad).reshape(source_total, D)
    out_wgrad = jnp.dot(relu_flat.T, grad_f, preferred_element_type=jnp.float32) / SH
    hidden = jnp.dot(grad_f, out_weight.astype(jnp.float32).T, preferred_element_type=jnp.float32).reshape(SH, SW, CH)
    block_grad = jnp.where(post_relu > 0, hidden, 0.0).astype(jnp.bfloat16)
    padded = jnp.pad(settle(block_grad), ((1, 1), (1, 1), (0, 0)))
    conv_f = conv_weight.astype(jnp.float32)
    input_f = conv_input.astype(jnp.float32)
    act_sum = jnp.zeros((SH, SW, CH), jnp.float32)
    tap_grads = []
    for row_tap in range(3):
        for col_tap in range(3):
            window = padded[2 - row_tap:2 - row_tap + SH, 2 - col_tap:2 - col_tap + SW]
            act_sum = act_sum + jnp.einsum('rwo,io->rwi', window, conv_f[row_tap, col_tap])
            tap_grads.append(jnp.einsum('rwi,rwo->io', input_f, window))
    conv_wgrad = jnp.stack(tap_grads).reshape(3, 3, CH, CH) / SH
    return (tgt_grad, act_sum.astype(jnp.bfloat16), out_wgrad, conv_wgrad)
```

```python
import math

import jax
import jax.numpy as jnp
from jax import lax
from jax.experimental import pallas as pl
from jax.experimental.pallas import tpu as pltpu
from jax.sharding import Mesh, PartitionSpec as P

SRC = ("zh", "x", "c")
TGT = ("y", "zl")
ALL = SRC + TGT
NEAR = ("c", "y", "zl")
FAR = ("zh", "x")


def corr_kernel(first_ref, grads_ref, cents_ref, corr_ref, wide, level_sums):
    row_no = pl.program_id(0)
    tgt_rows = 8
    lanes = corr_ref.shape[1]
    tgt_width = corr_ref.shape[0] // tgt_rows

    @pl.when(row_no == 0)
    def _():
        wide[...] = grads_ref[...].astype(jnp.float32)

    tile = (tgt_rows, lanes)
    center_y = jnp.broadcast_to(cents_ref[0, pl.ds(row_no, 1), :], tile)
    center_x = jnp.broadcast_to(cents_ref[1, pl.ds(row_no, 1), :], tile)
    ys = first_ref[0] + lax.broadcasted_iota(jnp.int32, tile, 0)
    zero = jnp.zeros(tile, jnp.float32)

    def spread(level):
        row_off = lax.shift_right_arithmetic(ys, level) - (
            lax.shift_right_arithmetic(center_y, level) - 4
        )
        hits = [row_off == a for a in range(9)]
        picked = []
        for b in range(9):
            acc = zero
            for a in range(9):
                entry = wide[81 * level + 9 * a + b, pl.ds(row_no, 1), :]
                acc = jnp.where(hits[a], jnp.broadcast_to(entry, tile), acc)
            picked.append(acc * (0.25**level) if level else acc)
        start = lax.shift_right_arithmetic(center_x, level) - 4
        turn = start & 15
        block = lax.shift_right_arithmetic(start, 4)
        slots = picked + [zero] * 7
        for bit in (8, 4, 2, 1):
            on = (turn & bit) != 0
            slots = [jnp.where(on, slots[(i - bit) % 16], slots[i]) for i in range(16)]
        homes = [jnp.where(turn > j, block + 1, block) for j in range(16)]
        return slots, homes

    offset = 0
    coarse = None
    for level in (3, 2, 1):
        slots, homes = spread(level)
        cells = tgt_width >> level
        for j in range(16):
            for q in range(cells // 16):
                x = 16 * q + j
                value = jnp.where(homes[j] == q, slots[j], 0.0)
                if coarse is not None:
                    value = value + level_sums[coarse + (x >> 1)]
                level_sums[offset + x] = value
        coarse = offset
        offset += cells
    slots, homes = spread(0)
    for j in range(0, 16, 2):
        for q in range(tgt_width // 16):
            x = 16 * q + j
            under = level_sums[coarse + (x >> 1)]
            left = jnp.where(homes[j] == q, slots[j], 0.0) + under
            right = jnp.where(homes[j + 1] == q, slots[j + 1], 0.0) + under
            pair = jnp.concatenate([left, right], axis=0).astype(jnp.bfloat16)
            corr_ref[x * tgt_rows : (x + 2) * tgt_rows, :] = pair


def corr_transposed(upstream, centers, row_first, tgt_rows, tgt_width):
    src_rows, src_width, lookups = upstream.shape
    grads = jnp.transpose(upstream, (2, 0, 1))
    return pl.pallas_call(
        corr_kernel,
        out_shape=jax.ShapeDtypeStruct((tgt_width * tgt_rows, src_rows * src_width), jnp.bfloat16),
        grid_spec=pltpu.PrefetchScalarGridSpec(
            num_scalar_prefetch=1,
            grid=(src_rows,),
            in_specs=[
                pl.BlockSpec((lookups, src_rows, src_width), lambda r, f: (0, 0, 0)),
                pl.BlockSpec((2, src_rows, src_width), lambda r, f: (0, 0, 0)),
            ],
            out_specs=pl.BlockSpec((tgt_width * tgt_rows, src_width), lambda r, f: (0, r)),
            scratch_shapes=[
                pltpu.VMEM((lookups, src_rows, src_width), jnp.float32),
                pltpu.VMEM((tgt_width, tgt_rows, src_width), jnp.float32),
            ],
        ),
        compiler_params=pltpu.CompilerParams(dimension_semantics=("arbitrary",)),
        cost_estimate=pl.CostEstimate(flops=20_000_000, bytes_accessed=6_000_000, transcendentals=0),
        name="corr_build",
    )(row_first.reshape(1), grads, centers)


def shares(value, axes):
    count = lax.axis_size(axes)
    return lax.all_to_all(jnp.broadcast_to(value[None], (count,) + value.shape), axes, 0, 0)


def summed(parts):
    return jnp.sum(parts.astype(jnp.float32), axis=0)


def moved(array, step):
    zero = jnp.zeros((1,) + array.shape[1:], array.dtype)
    if step > 0:
        return jnp.concatenate([zero, array[:-1]], axis=0)
    return jnp.concatenate([array[1:], zero], axis=0)


def body(upstream, centers, post_relu, conv_input, target_feats, out_weight, conv_weight):
    src_rows, src_width, lookups = upstream.shape
    tgt_rows, tgt_width, width = target_feats.shape
    chans = post_relu.shape[2]
    source_total = src_rows * src_width
    src_devices = lax.axis_size(SRC)
    row_total = src_devices * src_rows
    inv_root = 1.0 / math.sqrt(width)
    tgt_at = lax.axis_index(TGT)
    core_at = lax.axis_index("c")
    f32, bf16 = jnp.float32, jnp.bfloat16

    up = [(i, i + 1) for i in range(row_total - 1)]
    down = [(j, i) for i, j in up]
    own_input = conv_input[0]
    input_before = lax.ppermute(own_input, ALL, up)
    input_after = lax.ppermute(own_input, ALL, down)

    corr = corr_transposed(upstream, centers, tgt_at * tgt_rows, tgt_rows, tgt_width)
    targets = jnp.transpose(target_feats, (1, 0, 2)).reshape(tgt_width * tgt_rows, width)
    relu_flat = post_relu.reshape(source_total, chans)
    src_part = (
        lax.dot_general(corr, targets, (((0,), (0,)), ((), ())), preferred_element_type=f32)
        * inv_root
    ).astype(bf16)
    hidden = lax.dot_general(
        src_part, out_weight, (((1,), (1,)), ((), ())), preferred_element_type=f32
    ).astype(bf16)
    hidden = lax.all_to_all(hidden.reshape(src_rows, src_width, chans), TGT, 0, 0)
    out_term = lax.dot_general(
        relu_flat, src_part, (((0,), (0,)), ((), ())), preferred_element_type=f32
    )

    feats = jnp.dot(relu_flat, out_weight, preferred_element_type=f32).astype(bf16)
    tgt_part = (
        jnp.dot(corr, feats, preferred_element_type=f32) * inv_root
    ).astype(bf16)
    far = lax.axis_size(FAR)
    block = tgt_width // src_devices * tgt_rows
    tgt_part = tgt_part.reshape(far, 2, block, width)
    given = lax.dynamic_index_in_dim(tgt_part, 1 - core_at, 1, keepdims=False)
    kept = lax.dynamic_index_in_dim(tgt_part, core_at, 1, keepdims=False)
    swap = [
        (s * 8 + t, (s ^ 1) * 8 + t) for s in range(src_devices) for t in range(lax.axis_size(TGT))
    ]
    taken = lax.ppermute(given, ALL, swap)
    both = (kept.astype(f32) + taken.astype(f32)).astype(bf16)
    tgt_grad = summed(lax.all_to_all(both, FAR, 0, 0))
    tgt_grad = jnp.transpose(
        tgt_grad.reshape(tgt_width // src_devices, tgt_rows, width), (1, 0, 2)
    ).astype(bf16)

    own_relu = lax.dynamic_index_in_dim(post_relu, tgt_at, 0, keepdims=False)
    block_grad = jnp.where(own_relu > 0, summed(hidden), 0.0).astype(bf16)

    near_input = jnp.concatenate([input_before, own_input, input_after], axis=1)
    near_grad = jnp.concatenate([moved(block_grad, -1), block_grad, moved(block_grad, 1)], axis=1)
    conv_term = lax.dot_general(
        near_input, near_grad, (((0,), (0,)), ((), ())), preferred_element_type=f32
    )
    near = lax.axis_size(NEAR)
    terms = jnp.concatenate(
        [
            conv_term.astype(bf16).reshape(near, 3 * chans // near, 3 * chans),
            jnp.pad(
                out_term.astype(bf16).reshape(near, chans // near, width),
                ((0, 0), (0, 0), (0, 3 * chans - width)),
            ),
        ],
        axis=1,
    )
    piece = summed(lax.all_to_all(terms, NEAR, 0, 0)).astype(bf16)
    piece = (summed(shares(piece, FAR)) / row_total).astype(bf16)
    totals = shares(piece, NEAR).astype(f32)
    conv_total = totals[:, : 3 * chans // near].reshape(3, chans, 3, chans)
    conv_total = jnp.transpose(conv_total, (0, 2, 1, 3))
    out_total = totals[:, 3 * chans // near :, :width].reshape(chans, width)

    grad_before = lax.ppermute(block_grad, ALL, up)
    grad_after = lax.ppermute(block_grad, ALL, down)
    taps = []
    for row in (grad_after, block_grad, grad_before):
        taps += [moved(row, -1), row, moved(row, 1)]
    act_grad = lax.dot_general(
        jnp.concatenate(taps, axis=1),
        jnp.transpose(conv_weight, (0, 1, 3, 2)).reshape(9 * chans, chans),
        (((1,), (0,)), ((), ())),
        preferred_element_type=f32,
    ).astype(bf16)[None]
    return (tgt_grad, act_grad, out_total, conv_total)


def solution(mesh):
    grid = Mesh(mesh.devices.reshape(4, 4, 2, 4, 2), ALL)
    placed = (
        P(SRC, None, None),
        P(None, SRC, None),
        P(SRC, None, None),
        P(ALL, None, None),
        P(TGT, None, None),
        P(),
        P(),
    )
    return jax.shard_map(
        body,
        mesh=grid,
        in_specs=placed,
        out_specs=(P(TGT, SRC, None), P(ALL, None, None), P(), P()),
        check_vma=False,
    )
```

```python
import functools
import math

import jax
import jax.numpy as jnp
from jax import lax
from jax.experimental import pallas as pl
from jax.experimental.pallas import tpu as pltpu
from jax.sharding import Mesh, PartitionSpec as P


SRC = ("zh", "x", "c")
TGT = ("y", "zl")
ALL = SRC + TGT
NEAR = ("c", "y", "zl")
FAR = ("zh", "x")


def corr_kernel(
    first_ref,
    grads_ref,
    cents_ref,
    targets_ref,
    relu_ref,
    weight_ref,
    corr_ref,
    hidden_ref,
    out_ref,
    wide,
    level_sums,
    tall,
    targets,
):
    step_no = pl.program_id(0)
    tgt_rows, tgt_width, width = targets_ref.shape
    lanes = grads_ref.shape[2]
    pair_rows = corr_ref.shape[1] // lanes
    tile = (tgt_rows, lanes)

    @pl.when(step_no == 0)
    def _():
        wide[...] = grads_ref[...].astype(jnp.float32)
        for h in range(width // lanes):
            part = slice(h * lanes, (h + 1) * lanes)
            for y in range(tgt_rows):
                rows = targets_ref[y, :, part].astype(jnp.float32)
                tall[pl.ds(y, tgt_width, stride=tgt_rows), :] = rows
            targets[:, part] = tall[...].astype(jnp.bfloat16)
        out_ref[...] = jnp.zeros_like(out_ref)

    def build(half, carry):
        row_no = step_no * pair_rows + half
        at = pl.ds(pl.multiple_of(half * lanes, lanes), lanes)
        center_y = jnp.broadcast_to(cents_ref[0, pl.ds(row_no, 1), :], tile)
        center_x = jnp.broadcast_to(cents_ref[1, pl.ds(row_no, 1), :], tile)
        ys = first_ref[0] + lax.broadcasted_iota(jnp.int32, tile, 0)
        zero = jnp.zeros(tile, jnp.float32)

        def spread(level):
            row_off = lax.shift_right_arithmetic(ys, level) - (
                lax.shift_right_arithmetic(center_y, level) - 4
            )
            hits = [row_off == a for a in range(9)]
            picked = []
            for b in range(9):
                acc = zero
                for a in range(9):
                    entry = wide[81 * level + 9 * a + b, pl.ds(row_no, 1), :]
                    acc = jnp.where(hits[a], jnp.broadcast_to(entry, tile), acc)
                picked.append(acc * (0.25**level) if level else acc)
            start = lax.shift_right_arithmetic(center_x, level) - 4
            turn = start & 15
            block = lax.shift_right_arithmetic(start, 4)
            slots = picked + [zero] * 7
            for bit in (8, 4, 2, 1):
                on = (turn & bit) != 0
                slots = [jnp.where(on, slots[(i - bit) % 16], slots[i]) for i in range(16)]
            homes = [jnp.where(turn > j, block + 1, block) for j in range(16)]
            return slots, homes

        offset = 0
        coarse = None
        for level in (3, 2, 1):
            slots, homes = spread(level)
            cells = tgt_width >> level
            for j in range(16):
                for q in range(cells // 16):
                    x = 16 * q + j
                    value = jnp.where(homes[j] == q, slots[j], 0.0)
                    if coarse is not None:
                        value = value + level_sums[coarse + (x >> 1)]
                    level_sums[offset + x] = value
            coarse = offset
            offset += cells
        slots, homes = spread(0)
        for j in range(0, 16, 2):
            for q in range(tgt_width // 16):
                x = 16 * q + j
                under = level_sums[coarse + (x >> 1)]
                left = jnp.where(homes[j] == q, slots[j], 0.0) + under
                right = jnp.where(homes[j + 1] == q, slots[j + 1], 0.0) + under
                pair = jnp.concatenate([left, right], axis=0).astype(jnp.bfloat16)
                corr_ref[x * tgt_rows : (x + 2) * tgt_rows, at] = pair
        return carry

    lax.fori_loop(0, pair_rows, build, 0)
    src = lax.dot_general(
        corr_ref[...],
        targets[...],
        (((0,), (0,)), ((), ())),
        preferred_element_type=jnp.float32,
    )
    src = (src * (1.0 / math.sqrt(width))).astype(jnp.bfloat16)
    hidden = lax.dot_general(
        src, weight_ref[...], (((1,), (1,)), ((), ())), preferred_element_type=jnp.float32
    )
    hidden_ref[...] = hidden.astype(jnp.bfloat16)
    out_ref[...] += lax.dot_general(
        relu_ref[...], src, (((0,), (0,)), ((), ())), preferred_element_type=jnp.float32
    )


def source_pass(upstream, centers, relu_flat, target_feats, out_weight, row_first):
    src_rows, src_width, lookups = upstream.shape
    tgt_rows, tgt_width, width = target_feats.shape
    chans = relu_flat.shape[1]
    pair = 2 * src_width
    grads = jnp.transpose(upstream, (2, 0, 1))
    whole = lambda *shape: pl.BlockSpec(shape, lambda r, f: (0,) * len(shape))
    return pl.pallas_call(
        corr_kernel,
        out_shape=(
            jax.ShapeDtypeStruct((tgt_width * tgt_rows, src_rows * src_width), jnp.bfloat16),
            jax.ShapeDtypeStruct((src_rows * src_width, chans), jnp.bfloat16),
            jax.ShapeDtypeStruct((chans, width), jnp.float32),
        ),
        grid_spec=pltpu.PrefetchScalarGridSpec(
            num_scalar_prefetch=1,
            grid=(src_rows // 2,),
            in_specs=[
                whole(lookups, src_rows, src_width),
                whole(2, src_rows, src_width),
                whole(tgt_rows, tgt_width, width),
                pl.BlockSpec((pair, chans), lambda r, f: (r, 0)),
                whole(chans, width),
            ],
            out_specs=(
                pl.BlockSpec((tgt_width * tgt_rows, pair), lambda r, f: (0, r)),
                pl.BlockSpec((pair, chans), lambda r, f: (r, 0)),
                whole(chans, width),
            ),
            scratch_shapes=[
                pltpu.VMEM((lookups, src_rows, src_width), jnp.float32),
                pltpu.VMEM((tgt_width, tgt_rows, src_width), jnp.float32),
                pltpu.VMEM((tgt_width * tgt_rows, src_width), jnp.float32),
                pltpu.VMEM((tgt_width * tgt_rows, width), jnp.bfloat16),
            ],
        ),
        compiler_params=pltpu.CompilerParams(dimension_semantics=("arbitrary",)),
        cost_estimate=pl.CostEstimate(
            flops=4_000_000_000, bytes_accessed=7_000_000, transcendentals=0
        ),
        name="source_pass",
    )(row_first.reshape(1), grads, centers, target_feats, relu_flat, out_weight)


def target_kernel(core_ref, corr_ref, relu_ref, weight_ref, given_ref, kept_ref, feats):
    @pl.when(pl.program_id(0) == 0)
    def _():
        feats[...] = jnp.dot(
            relu_ref[...], weight_ref[...], preferred_element_type=jnp.float32
        ).astype(jnp.bfloat16)

    count, block, width = given_ref.shape
    part = jnp.dot(corr_ref[...], feats[...], preferred_element_type=jnp.float32)
    part = (part * (1.0 / math.sqrt(width))).astype(jnp.bfloat16).reshape(count, 2, block, width)
    first = core_ref[0] == 0

    @pl.when(first)
    def _():
        given_ref[...] = part[:, 1]
        kept_ref[...] = part[:, 0]

    @pl.when(jnp.logical_not(first))
    def _():
        given_ref[...] = part[:, 0]
        kept_ref[...] = part[:, 1]


def target_pass(corr, relu_flat, out_weight, core_at, far, block):
    cells, sources = corr.shape
    chans, width = out_weight.shape
    steps = 4
    whole = lambda *shape: pl.BlockSpec(shape, lambda r, f: (0,) * len(shape))
    part = pl.BlockSpec((far // steps, block, width), lambda r, f: (r, 0, 0))
    return pl.pallas_call(
        target_kernel,
        out_shape=(jax.ShapeDtypeStruct((far, block, width), jnp.bfloat16),) * 2,
        grid_spec=pltpu.PrefetchScalarGridSpec(
            num_scalar_prefetch=1,
            grid=(steps,),
            in_specs=[
                pl.BlockSpec((cells // steps, sources), lambda r, f: (r, 0)),
                whole(sources, chans),
                whole(chans, width),
            ],
            out_specs=(part, part),
            scratch_shapes=[pltpu.VMEM((sources, width), jnp.bfloat16)],
        ),
        compiler_params=pltpu.CompilerParams(dimension_semantics=("arbitrary",)),
        cost_estimate=pl.CostEstimate(
            flops=2 * cells * sources * width, bytes_accessed=6_500_000, transcendentals=0
        ),
        name="target_pass",
    )(core_at.reshape(1), corr, relu_flat, out_weight)


def terms_kernel(tgt_ref, parts_ref, relu_ref, before_ref, own_ref, after_ref, out_ref, grad_ref, terms_ref):
    total = parts_ref[0].astype(jnp.float32)
    for k in range(1, parts_ref.shape[0]):
        total += parts_ref[k].astype(jnp.float32)
    grad = jnp.where(relu_ref[0].astype(jnp.float32) > 0, total, 0.0).astype(jnp.bfloat16)
    grad_ref[...] = grad
    wide = grad.astype(jnp.float32)
    count = wide.shape[0]
    rows = lax.broadcasted_iota(jnp.int32, wide.shape, 0)
    left = jnp.where(rows == count - 1, 0.0, pltpu.roll(wide, count - 1, 0))
    right = jnp.where(rows == 0, 0.0, pltpu.roll(wide, 1, 0))
    near_grad = jnp.concatenate([left, wide, right], axis=1).astype(jnp.bfloat16)
    near_input = jnp.concatenate([before_ref[...], own_ref[...], after_ref[...]], axis=1)
    conv = lax.dot_general(
        near_input, near_grad, (((0,), (0,)), ((), ())), preferred_element_type=jnp.float32
    )
    near, _, across = terms_ref.shape
    chans, width = out_ref.shape
    out = jnp.concatenate(
        [out_ref[...], jnp.zeros((chans, across - width), jnp.float32)], axis=1
    )
    terms_ref[...] = jnp.concatenate(
        [
            conv.reshape(near, conv.shape[0] // near, across),
            out.reshape(near, chans // near, across),
        ],
        axis=1,
    ).astype(jnp.bfloat16)


def weight_terms(parts, post_relu, inputs, out_term, tgt_at, near):
    count, src_width, chans = parts.shape
    width = out_term.shape[1]
    whole = lambda *shape: pl.BlockSpec(shape, lambda r, f: (0,) * len(shape))
    across = 3 * chans
    down = (across + chans) // near
    return pl.pallas_call(
        terms_kernel,
        out_shape=(
            jax.ShapeDtypeStruct((src_width, chans), jnp.bfloat16),
            jax.ShapeDtypeStruct((near, down, across), jnp.bfloat16),
        ),
        grid_spec=pltpu.PrefetchScalarGridSpec(
            num_scalar_prefetch=1,
            grid=(1,),
            in_specs=[
                whole(count, src_width, chans),
                pl.BlockSpec((1, src_width, chans), lambda r, f: (f[0], 0, 0)),
                whole(src_width, chans),
                whole(src_width, chans),
                whole(src_width, chans),
                whole(chans, width),
            ],
            out_specs=(whole(src_width, chans), whole(near, down, across)),
        ),
        compiler_params=pltpu.CompilerParams(vmem_limit_bytes=8 * 2**20),
        name="weight_terms",
    )(tgt_at.reshape(1), parts, post_relu, *inputs, out_term)


def near_sum_kernel(parts_ref, kept_ref, taken_ref, joint_ref):
    total = parts_ref[0].astype(jnp.float32)
    for k in range(1, parts_ref.shape[0]):
        total += parts_ref[k].astype(jnp.float32)
    rows = total.shape[0]
    last = total[:, 256:]
    total = jnp.concatenate(
        [total[:, :256], jnp.concatenate([last[: rows // 2], last[rows // 2 :]], axis=1)], axis=0
    ).astype(jnp.bfloat16)
    block = kept_ref.shape[1]
    for k in range(joint_ref.shape[0]):
        both = kept_ref[k].astype(jnp.float32) + taken_ref[k].astype(jnp.float32)
        joint_ref[k, :block] = both.astype(jnp.bfloat16)
        joint_ref[k, block:] = total


def near_sum(parts, kept, taken):
    far, block, width = kept.shape
    return pl.pallas_call(
        near_sum_kernel,
        out_shape=jax.ShapeDtypeStruct(
            (far, block + parts.shape[1] * parts.shape[2] // width, width), jnp.bfloat16
        ),
        compiler_params=pltpu.CompilerParams(vmem_limit_bytes=8 * 2**20),
        name="near_sum",
    )(parts, kept, taken)


def far_sum_kernel(scale, parts_ref, tgt_ref, shared_ref, left, right):
    total = parts_ref[0].astype(jnp.float32)
    for k in range(1, parts_ref.shape[0]):
        total += parts_ref[k].astype(jnp.float32)
    tgt_rows, cols, width = tgt_ref.shape
    block = tgt_rows * cols
    near, rows, _ = shared_ref.shape
    left[...] = total[:block, : width // 2]
    right[...] = total[:block, width // 2 :]
    for y in range(tgt_rows):
        at = pl.ds(y, cols, stride=tgt_rows)
        row = jnp.concatenate([left[at, :], right[at, :]], axis=1)
        tgt_ref[y] = row.astype(jnp.bfloat16)
    first = total[block : block + rows]
    second = total[block + rows :]
    second = jnp.concatenate([second[:, : width // 2], second[:, width // 2 :]], axis=0)
    piece = (jnp.concatenate([first, second], axis=1) * scale).astype(jnp.bfloat16)
    for k in range(near):
        shared_ref[k] = piece


def far_sum(parts, tgt_rows, cols, near, rows, across, scale):
    width = parts.shape[2]
    return pl.pallas_call(
        functools.partial(far_sum_kernel, scale),
        out_shape=(
            jax.ShapeDtypeStruct((tgt_rows, cols, width), jnp.bfloat16),
            jax.ShapeDtypeStruct((near, rows, across), jnp.bfloat16),
        ),
        scratch_shapes=[pltpu.VMEM((tgt_rows * cols, width // 2), jnp.float32)] * 2,
        compiler_params=pltpu.CompilerParams(vmem_limit_bytes=8 * 2**20),
        name="far_sum",
    )(parts)


def unpack_kernel(totals_ref, conv_ref, out_ref):
    totals = totals_ref[...].astype(jnp.float32)
    near, _, across = totals.shape
    chans, width = out_ref.shape
    depth = across // near
    conv = totals[:, :depth, :].reshape(across, across)
    for p in range(3):
        for q in range(3):
            conv_ref[p, q] = conv[p * chans : (p + 1) * chans, q * chans : (q + 1) * chans]
    out_ref[...] = totals[:, depth:, :width].reshape(chans, width)


def unpack(totals, chans, width):
    return pl.pallas_call(
        unpack_kernel,
        out_shape=(
            jax.ShapeDtypeStruct((3, 3, chans, chans), jnp.float32),
            jax.ShapeDtypeStruct((chans, width), jnp.float32),
        ),
        compiler_params=pltpu.CompilerParams(vmem_limit_bytes=8 * 2**20),
        name="unpack",
    )(totals)


def moved(array, step):
    zero = jnp.zeros((1,) + array.shape[1:], array.dtype)
    if step > 0:
        return jnp.concatenate([zero, array[:-1]], axis=0)
    return jnp.concatenate([array[1:], zero], axis=0)


def body(upstream, centers, post_relu, conv_input, target_feats, out_weight, conv_weight):
    src_rows, src_width, _ = upstream.shape
    tgt_rows, tgt_width, width = target_feats.shape
    chans = post_relu.shape[2]
    source_total = src_rows * src_width
    src_devices = lax.axis_size(SRC)
    tgt_devices = lax.axis_size(TGT)
    row_total = src_devices * src_rows
    near, far = lax.axis_size(NEAR), lax.axis_size(FAR)
    tgt_at = lax.axis_index(TGT)
    core_at = lax.axis_index("c")
    f32, bf16 = jnp.float32, jnp.bfloat16

    up = [(i, i + 1) for i in range(row_total - 1)]
    down = [(j, i) for i, j in up]
    own_input = conv_input[0]
    input_before = lax.ppermute(own_input, ALL, up)
    input_after = lax.ppermute(own_input, ALL, down)

    relu_flat = post_relu.reshape(source_total, chans)
    corr, hidden, out_term = source_pass(
        upstream, centers, relu_flat, target_feats, out_weight, tgt_at * tgt_rows
    )
    hidden = lax.all_to_all(hidden.reshape(src_rows, src_width, chans), TGT, 0, 0)

    block = tgt_width // src_devices * tgt_rows
    given, kept = target_pass(corr, relu_flat, out_weight, core_at, far, block)
    swap = [(s * tgt_devices + t, (s ^ 1) * tgt_devices + t) for s in range(src_devices) for t in range(tgt_devices)]
    taken = lax.ppermute(given, ALL, swap)
    block_grad, terms = weight_terms(
        hidden, post_relu, (input_before, own_input, input_after), out_term, tgt_at, near
    )
    terms = lax.all_to_all(terms, NEAR, 0, 0)
    grad_before = lax.ppermute(block_grad, ALL, up)
    grad_after = lax.ppermute(block_grad, ALL, down)
    joint = near_sum(terms, kept, taken)
    joint = lax.all_to_all(joint, FAR, 0, 0)
    tgt_grad, pieces = far_sum(
        joint, tgt_rows, tgt_width // src_devices, near, terms.shape[1], terms.shape[2], 1.0 / row_total
    )
    pieces = lax.all_to_all(pieces, NEAR, 0, 0)
    conv_total, out_total = unpack(pieces, chans, width)

    taps = []
    for row in (grad_after, block_grad, grad_before):
        taps += [moved(row, -1), row, moved(row, 1)]
    act_grad = lax.dot_general(
        jnp.concatenate(taps, axis=1),
        jnp.transpose(conv_weight, (0, 1, 3, 2)).reshape(9 * chans, chans),
        (((1,), (0,)), ((), ())),
        preferred_element_type=f32,
    ).astype(bf16)[None]
    return (tgt_grad, act_grad, out_total, conv_total)


def solution(mesh):
    grid = Mesh(mesh.devices.reshape(4, 4, 2, 4, 2), ALL)
    placed = (
        P(SRC, None, None),
        P(None, SRC, None),
        P(SRC, None, None),
        P(ALL, None, None),
        P(TGT, None, None),
        P(),
        P(),
    )
    return jax.shard_map(
        body,
        mesh=grid,
        in_specs=placed,
        out_specs=(P(TGT, SRC, None), P(ALL, None, None), P(), P()),
        check_vma=False,
    )
```

```python
import functools
import math

import jax
import jax.numpy as jnp
from jax import lax
from jax.experimental import pallas as pl
from jax.experimental.pallas import tpu as pltpu
from jax.sharding import Mesh, PartitionSpec as P


SRC = ("zh", "x", "c")
TGT = ("y", "zl")
ALL = SRC + TGT
NEAR = ("c", "y", "zl")


def corr_kernel(
    first_ref,
    grads_ref,
    cents_ref,
    targets_ref,
    relu_ref,
    weight_ref,
    corr_ref,
    hidden_ref,
    out_ref,
    wide,
    level_sums,
    tall,
    targets,
):
    step_no = pl.program_id(0)
    tgt_rows, tgt_width, width = targets_ref.shape
    lanes = grads_ref.shape[2]
    pair_rows = corr_ref.shape[1] // lanes
    tile = (tgt_rows, lanes)

    @pl.when(step_no == 0)
    def _():
        wide[...] = grads_ref[...].astype(jnp.float32)
        for h in range(width // lanes):
            part = slice(h * lanes, (h + 1) * lanes)
            for y in range(tgt_rows):
                rows = targets_ref[y, :, part].astype(jnp.float32)
                tall[pl.ds(y, tgt_width, stride=tgt_rows), :] = rows
            targets[:, part] = tall[...].astype(jnp.bfloat16)
        out_ref[...] = jnp.zeros_like(out_ref)

    def build(half, carry):
        row_no = step_no * pair_rows + half
        at = pl.ds(pl.multiple_of(half * lanes, lanes), lanes)
        center_y = jnp.broadcast_to(cents_ref[0, pl.ds(row_no, 1), :], tile)
        center_x = jnp.broadcast_to(cents_ref[1, pl.ds(row_no, 1), :], tile)
        ys = first_ref[0] + lax.broadcasted_iota(jnp.int32, tile, 0)
        zero = jnp.zeros(tile, jnp.float32)

        def spread(level):
            row_off = lax.shift_right_arithmetic(ys, level) - (
                lax.shift_right_arithmetic(center_y, level) - 4
            )
            hits = [row_off == a for a in range(9)]
            picked = []
            for b in range(9):
                acc = zero
                for a in range(9):
                    entry = wide[81 * level + 9 * a + b, pl.ds(row_no, 1), :]
                    acc = jnp.where(hits[a], jnp.broadcast_to(entry, tile), acc)
                picked.append(acc * (0.25**level) if level else acc)
            start = lax.shift_right_arithmetic(center_x, level) - 4
            turn = start & 15
            block = lax.shift_right_arithmetic(start, 4)
            slots = picked + [zero] * 7
            for bit in (8, 4, 2, 1):
                on = (turn & bit) != 0
                slots = [jnp.where(on, slots[(i - bit) % 16], slots[i]) for i in range(16)]
            homes = [jnp.where(turn > j, block + 1, block) for j in range(16)]
            return slots, homes

        offset = 0
        coarse = None
        for level in (3, 2, 1):
            slots, homes = spread(level)
            cells = tgt_width >> level
            for j in range(16):
                for q in range(cells // 16):
                    x = 16 * q + j
                    value = jnp.where(homes[j] == q, slots[j], 0.0)
                    if coarse is not None:
                        value = value + level_sums[coarse + (x >> 1)]
                    level_sums[offset + x] = value
            coarse = offset
            offset += cells
        slots, homes = spread(0)
        for j in range(0, 16, 2):
            for q in range(tgt_width // 16):
                x = 16 * q + j
                under = level_sums[coarse + (x >> 1)]
                left = jnp.where(homes[j] == q, slots[j], 0.0) + under
                right = jnp.where(homes[j + 1] == q, slots[j + 1], 0.0) + under
                pair = jnp.concatenate([left, right], axis=0).astype(jnp.bfloat16)
                corr_ref[x * tgt_rows : (x + 2) * tgt_rows, at] = pair
        return carry

    lax.fori_loop(0, pair_rows, build, 0)
    src = lax.dot_general(
        corr_ref[...],
        targets[...],
        (((0,), (0,)), ((), ())),
        preferred_element_type=jnp.float32,
    )
    exact = src * (1.0 / math.sqrt(width))
    src = exact.astype(jnp.bfloat16)
    rest = (exact - src.astype(jnp.float32)).astype(jnp.bfloat16)
    across = (((1,), (1,)), ((), ()))
    hidden = lax.dot_general(
        src, weight_ref[...], across, preferred_element_type=jnp.float32
    ) + lax.dot_general(rest, weight_ref[...], across, preferred_element_type=jnp.float32)
    hidden_ref[...] = hidden.astype(jnp.bfloat16)
    out_ref[...] += lax.dot_general(
        relu_ref[...], src, (((0,), (0,)), ((), ())), preferred_element_type=jnp.float32
    )


def source_pass(upstream, centers, relu_flat, target_feats, out_weight, row_first):
    src_rows, src_width, lookups = upstream.shape
    tgt_rows, tgt_width, width = target_feats.shape
    chans = relu_flat.shape[1]
    pair = 2 * src_width
    grads = jnp.transpose(upstream, (2, 0, 1))
    whole = lambda *shape: pl.BlockSpec(shape, lambda r, f: (0,) * len(shape))
    return pl.pallas_call(
        corr_kernel,
        out_shape=(
            jax.ShapeDtypeStruct((tgt_width * tgt_rows, src_rows * src_width), jnp.bfloat16),
            jax.ShapeDtypeStruct((src_rows * src_width, chans), jnp.bfloat16),
            jax.ShapeDtypeStruct((chans, width), jnp.float32),
        ),
        grid_spec=pltpu.PrefetchScalarGridSpec(
            num_scalar_prefetch=1,
            grid=(src_rows // 2,),
            in_specs=[
                whole(lookups, src_rows, src_width),
                whole(2, src_rows, src_width),
                whole(tgt_rows, tgt_width, width),
                pl.BlockSpec((pair, chans), lambda r, f: (r, 0)),
                whole(chans, width),
            ],
            out_specs=(
                pl.BlockSpec((tgt_width * tgt_rows, pair), lambda r, f: (0, r)),
                pl.BlockSpec((pair, chans), lambda r, f: (r, 0)),
                whole(chans, width),
            ),
            scratch_shapes=[
                pltpu.VMEM((lookups, src_rows, src_width), jnp.float32),
                pltpu.VMEM((tgt_width, tgt_rows, src_width), jnp.float32),
                pltpu.VMEM((tgt_width * tgt_rows, src_width), jnp.float32),
                pltpu.VMEM((tgt_width * tgt_rows, width), jnp.bfloat16),
            ],
        ),
        compiler_params=pltpu.CompilerParams(dimension_semantics=("arbitrary",)),
        cost_estimate=pl.CostEstimate(
            flops=4_000_000_000, bytes_accessed=7_000_000, transcendentals=0
        ),
        name="source_pass",
    )(row_first.reshape(1), grads, centers, target_feats, relu_flat, out_weight)


def target_kernel(core_ref, corr_ref, relu_ref, weight_ref, given_ref, kept_ref, feats):
    @pl.when(pl.program_id(0) == 0)
    def _():
        feats[...] = jnp.dot(
            relu_ref[...], weight_ref[...], preferred_element_type=jnp.float32
        ).astype(jnp.bfloat16)

    highs, _, both, sources = corr_ref.shape
    width = given_ref.shape[2]
    block = both // 2
    part = jnp.dot(
        corr_ref[...].reshape(highs * both, sources),
        feats[...],
        preferred_element_type=jnp.float32,
    )
    part = (part * (1.0 / math.sqrt(width))).astype(jnp.bfloat16).reshape(highs, 2, block, width)
    rows = highs * block
    first = core_ref[0] == 0

    @pl.when(first)
    def _():
        given_ref[0] = part[:, 1].reshape(rows, width)
        kept_ref[0] = part[:, 0].reshape(rows, width)

    @pl.when(jnp.logical_not(first))
    def _():
        given_ref[0] = part[:, 0].reshape(rows, width)
        kept_ref[0] = part[:, 1].reshape(rows, width)


def target_pass(corr, relu_flat, out_weight, core_at, highs, steps):
    cells, sources = corr.shape
    chans, width = out_weight.shape
    rows = cells // steps // 2
    whole = lambda *shape: pl.BlockSpec(shape, lambda r, f: (0,) * len(shape))
    part = pl.BlockSpec((1, rows, width), lambda r, f: (r, 0, 0))
    both = cells // steps // highs
    return pl.pallas_call(
        target_kernel,
        out_shape=(jax.ShapeDtypeStruct((steps, rows, width), jnp.bfloat16),) * 2,
        grid_spec=pltpu.PrefetchScalarGridSpec(
            num_scalar_prefetch=1,
            grid=(steps,),
            in_specs=[
                pl.BlockSpec((highs, 1, both, sources), lambda r, f: (0, r, 0, 0)),
                whole(sources, chans),
                whole(chans, width),
            ],
            out_specs=(part, part),
            scratch_shapes=[pltpu.VMEM((sources, width), jnp.bfloat16)],
        ),
        compiler_params=pltpu.CompilerParams(dimension_semantics=("arbitrary",)),
        cost_estimate=pl.CostEstimate(
            flops=2 * cells * sources * width, bytes_accessed=6_500_000, transcendentals=0
        ),
        name="target_pass",
    )(core_at.reshape(1), corr.reshape(highs, steps, both, sources), relu_flat, out_weight)


def shifted(wide):
    count = wide.shape[0]
    rows = lax.broadcasted_iota(jnp.int32, wide.shape, 0)
    left = jnp.where(rows == count - 1, 0.0, pltpu.roll(wide, count - 1, 0))
    right = jnp.where(rows == 0, 0.0, pltpu.roll(wide, 1, 0))
    return left, wide, right


def terms_kernel(at_ref, parts_ref, relu_ref, paired_ref, own_ref, linked_ref, out_ref, grad_ref, terms_ref):
    total = parts_ref[0].astype(jnp.float32)
    for k in range(1, parts_ref.shape[0]):
        total += parts_ref[k].astype(jnp.float32)
    grad = jnp.where(relu_ref[0].astype(jnp.float32) > 0, total, 0.0).astype(jnp.bfloat16)
    grad_ref[...] = grad
    near_grad = jnp.concatenate(shifted(grad.astype(jnp.float32)), axis=1).astype(jnp.bfloat16)
    even = at_ref[1] == 0
    before = jnp.where(even, linked_ref[...], paired_ref[...])
    after = jnp.where(even, paired_ref[...], linked_ref[...])
    near_input = jnp.concatenate([before, own_ref[...], after], axis=1)
    conv = lax.dot_general(
        near_input, near_grad, (((0,), (0,)), ((), ())), preferred_element_type=jnp.float32
    )
    near, _, across = terms_ref.shape
    chans, width = out_ref.shape
    out = jnp.concatenate(
        [out_ref[...], jnp.zeros((chans, across - width), jnp.float32)], axis=1
    )
    terms_ref[...] = jnp.concatenate(
        [
            conv.reshape(near, conv.shape[0] // near, across),
            out.reshape(near, chans // near, across),
        ],
        axis=1,
    ).astype(jnp.bfloat16)


def weight_terms(parts, post_relu, inputs, out_term, tgt_at, odd, near):
    count, src_width, chans = parts.shape
    width = out_term.shape[1]
    whole = lambda *shape: pl.BlockSpec(shape, lambda r, f: (0,) * len(shape))
    across = 3 * chans
    down = (across + chans) // near
    return pl.pallas_call(
        terms_kernel,
        out_shape=(
            jax.ShapeDtypeStruct((src_width, chans), jnp.bfloat16),
            jax.ShapeDtypeStruct((near, down, across), jnp.bfloat16),
        ),
        grid_spec=pltpu.PrefetchScalarGridSpec(
            num_scalar_prefetch=1,
            grid=(1,),
            in_specs=[
                whole(count, src_width, chans),
                pl.BlockSpec((1, src_width, chans), lambda r, f: (f[0], 0, 0)),
                whole(src_width, chans),
                whole(src_width, chans),
                whole(src_width, chans),
                whole(chans, width),
            ],
            out_specs=(whole(src_width, chans), whole(near, down, across)),
        ),
        compiler_params=pltpu.CompilerParams(vmem_limit_bytes=8 * 2**20),
        name="weight_terms",
    )(jnp.stack([tgt_at, odd]), parts, post_relu, *inputs, out_term)


def near_sum_kernel(parts_ref, kept_ref, taken_ref, joint_ref):
    total = parts_ref[0].astype(jnp.float32)
    for k in range(1, parts_ref.shape[0]):
        total += parts_ref[k].astype(jnp.float32)
    rows = total.shape[0]
    width = joint_ref.shape[2]
    last = total[:, width:]
    total = jnp.concatenate(
        [total[:, :width], jnp.concatenate([last[: rows // 2], last[rows // 2 :]], axis=1)], axis=0
    ).astype(jnp.bfloat16)
    block = kept_ref.shape[1]
    for k in range(joint_ref.shape[0]):
        both = kept_ref[k].astype(jnp.float32) + taken_ref[k].astype(jnp.float32)
        joint_ref[k, :block] = both.astype(jnp.bfloat16)
        joint_ref[k, block:] = total


def near_sum(parts, kept, taken):
    count, block, width = kept.shape
    return pl.pallas_call(
        near_sum_kernel,
        out_shape=jax.ShapeDtypeStruct(
            (count, block + parts.shape[1] * parts.shape[2] // width, width), jnp.bfloat16
        ),
        compiler_params=pltpu.CompilerParams(vmem_limit_bytes=8 * 2**20),
        name="near_sum",
    )(parts, kept, taken)


def x_sum_kernel(parts_ref, joint_ref):
    total = parts_ref[0].astype(jnp.float32)
    for k in range(1, parts_ref.shape[0]):
        total += parts_ref[k].astype(jnp.float32)
    total = total.astype(jnp.bfloat16)
    count, rows, _ = joint_ref.shape
    piece = (count * rows - total.shape[0]) // (count - 1)
    block = rows - piece
    for k in range(count):
        joint_ref[k, :block] = total[k * block : (k + 1) * block]
        joint_ref[k, block:] = total[count * block :]


def x_sum(parts, count, block):
    _, rows, width = parts.shape
    return pl.pallas_call(
        x_sum_kernel,
        out_shape=jax.ShapeDtypeStruct(
            (count, block + rows - count * block, width), jnp.bfloat16
        ),
        compiler_params=pltpu.CompilerParams(vmem_limit_bytes=8 * 2**20),
        name="x_sum",
    )(parts)


def act_kernel(at_ref, grad_ref, paired_ref, linked_ref, weight_ref, act_ref):
    even = at_ref[0] == 0
    before = jnp.where(even, linked_ref[...], paired_ref[...])
    after = jnp.where(even, paired_ref[...], linked_ref[...])
    total = jnp.zeros(grad_ref.shape, jnp.float32)
    for p, row in enumerate((after, grad_ref[...], before)):
        for q, tap in enumerate(shifted(row.astype(jnp.float32))):
            total += lax.dot_general(
                tap.astype(jnp.bfloat16),
                weight_ref[p, q],
                (((1,), (1,)), ((), ())),
                preferred_element_type=jnp.float32,
            )
    act_ref[0] = total.astype(jnp.bfloat16)


def act_rows(block_grad, paired, linked, conv_weight, odd):
    whole = lambda *shape: pl.BlockSpec(shape, lambda r, f: (0,) * len(shape))
    cols, chans = block_grad.shape
    row = whole(cols, chans)
    return pl.pallas_call(
        act_kernel,
        out_shape=jax.ShapeDtypeStruct((1, cols, chans), jnp.bfloat16),
        grid_spec=pltpu.PrefetchScalarGridSpec(
            num_scalar_prefetch=1,
            grid=(1,),
            in_specs=[row, row, row, whole(3, 3, chans, chans)],
            out_specs=whole(1, cols, chans),
        ),
        compiler_params=pltpu.CompilerParams(vmem_limit_bytes=8 * 2**20),
        name="act_rows",
    )(odd.reshape(1), block_grad, paired, linked, conv_weight)


def far_sum_kernel(scale, parts_ref, tgt_ref, shared_ref, left, right):
    total = parts_ref[0].astype(jnp.float32)
    for k in range(1, parts_ref.shape[0]):
        total += parts_ref[k].astype(jnp.float32)
    tgt_rows, cols, width = tgt_ref.shape
    block = tgt_rows * cols
    near, rows, _ = shared_ref.shape
    left[...] = total[:block, : width // 2]
    right[...] = total[:block, width // 2 :]
    for y in range(tgt_rows):
        at = pl.ds(y, cols, stride=tgt_rows)
        row = jnp.concatenate([left[at, :], right[at, :]], axis=1)
        tgt_ref[y] = row.astype(jnp.bfloat16)
    first = total[block : block + rows]
    second = total[block + rows :]
    second = jnp.concatenate([second[:, : width // 2], second[:, width // 2 :]], axis=0)
    piece = (jnp.concatenate([first, second], axis=1) * scale).astype(jnp.bfloat16)
    for k in range(near):
        shared_ref[k] = piece


def far_sum(parts, tgt_rows, cols, near, rows, across, scale):
    width = parts.shape[2]
    return pl.pallas_call(
        functools.partial(far_sum_kernel, scale),
        out_shape=(
            jax.ShapeDtypeStruct((tgt_rows, cols, width), jnp.bfloat16),
            jax.ShapeDtypeStruct((near, rows, across), jnp.bfloat16),
        ),
        scratch_shapes=[pltpu.VMEM((tgt_rows * cols, width // 2), jnp.float32)] * 2,
        compiler_params=pltpu.CompilerParams(vmem_limit_bytes=8 * 2**20),
        name="far_sum",
    )(parts)


def unpack_kernel(totals_ref, conv_ref, out_ref):
    totals = totals_ref[...].astype(jnp.float32)
    near, _, across = totals.shape
    chans, width = out_ref.shape
    depth = across // near
    conv = totals[:, :depth, :].reshape(across, across)
    for p in range(3):
        for q in range(3):
            conv_ref[p, q] = conv[p * chans : (p + 1) * chans, q * chans : (q + 1) * chans]
    out_ref[...] = totals[:, depth:, :width].reshape(chans, width)


def unpack(totals, chans, width):
    return pl.pallas_call(
        unpack_kernel,
        out_shape=(
            jax.ShapeDtypeStruct((3, 3, chans, chans), jnp.float32),
            jax.ShapeDtypeStruct((chans, width), jnp.float32),
        ),
        compiler_params=pltpu.CompilerParams(vmem_limit_bytes=8 * 2**20),
        name="unpack",
    )(totals)


def body(upstream, centers, post_relu, conv_input, target_feats, out_weight, conv_weight):
    src_rows, src_width, _ = upstream.shape
    tgt_rows, tgt_width, width = target_feats.shape
    chans = post_relu.shape[2]
    src_devices = lax.axis_size(SRC)
    row_total = src_devices * src_rows
    near, highs, lows = lax.axis_size(NEAR), lax.axis_size("zh"), lax.axis_size("x")
    tgt_at = lax.axis_index(TGT)
    core_at = lax.axis_index("c")
    odd = lax.axis_index("zl")

    pairs = [(i, i ^ 1) for i in range(row_total)]
    links = [(i, i + 1) for i in range(1, row_total - 1, 2)]
    links += [(j, i) for i, j in links]
    own_input = conv_input[0]
    input_paired = lax.ppermute(own_input, ALL, pairs)
    input_linked = lax.ppermute(own_input, ALL, links)

    relu_flat = post_relu.reshape(src_rows * src_width, chans)
    corr, hidden, out_term = source_pass(
        upstream, centers, relu_flat, target_feats, out_weight, tgt_at * tgt_rows
    )
    hidden = lax.all_to_all(hidden.reshape(src_rows, src_width, chans), TGT, 0, 0)

    given, kept = target_pass(corr, relu_flat, out_weight, core_at, highs, lows)
    taken = lax.ppermute(given, "c", [(0, 1), (1, 0)])

    block_grad, terms = weight_terms(
        hidden, post_relu, (input_paired, own_input, input_linked), out_term, tgt_at, odd, near
    )
    terms = lax.all_to_all(terms, NEAR, 0, 0)
    grad_paired = lax.ppermute(block_grad, ALL, pairs)
    grad_linked = lax.ppermute(block_grad, ALL, links)
    joint = near_sum(terms, kept, taken)
    joint = lax.all_to_all(joint, "x", 0, 0)
    cols = tgt_width // src_devices
    joint = x_sum(joint, highs, cols * tgt_rows)
    joint = lax.all_to_all(joint, "zh", 0, 0)
    tgt_grad, pieces = far_sum(
        joint, tgt_rows, cols, near, terms.shape[1], terms.shape[2], 1.0 / row_total
    )
    pieces = lax.all_to_all(pieces, NEAR, 0, 0)
    act_grad = act_rows(block_grad, grad_paired, grad_linked, conv_weight, odd)
    conv_total, out_total = unpack(pieces, chans, width)
    return (tgt_grad, act_grad, out_total, conv_total)


def solution(mesh):
    grid = Mesh(mesh.devices.reshape(4, 4, 2, 4, 2), ALL)
    placed = (
        P(SRC, None, None),
        P(None, SRC, None),
        P(SRC, None, None),
        P(ALL, None, None),
        P(TGT, None, None),
        P(),
        P(),
    )
    return jax.shard_map(
        body,
        mesh=grid,
        in_specs=placed,
        out_specs=(P(TGT, SRC, None), P(ALL, None, None), P(), P()),
        check_vma=False,
    )
```

```python
import functools
import math

import jax
import jax.numpy as jnp
from jax import lax
from jax.experimental import pallas as pl
from jax.experimental.pallas import tpu as pltpu
from jax.sharding import Mesh, PartitionSpec as P


SRC = ("zh", "x", "c")
TGT = ("y", "zl")
ALL = SRC + TGT
NEAR = ("c", "y", "zl")


def corr_kernel(
    first_ref,
    grads_ref,
    cents_ref,
    targets_ref,
    relu_ref,
    weight_ref,
    corr_ref,
    hidden_ref,
    out_ref,
    wide,
    level_sums,
    tall,
    targets,
):
    step_no = pl.program_id(0)
    tgt_rows, tgt_width, width = targets_ref.shape
    lanes = grads_ref.shape[2]
    pair_rows = corr_ref.shape[1] // lanes
    tile = (tgt_rows, lanes)

    @pl.when(step_no == 0)
    def _():
        wide[...] = grads_ref[...].astype(jnp.float32)
        for h in range(width // lanes):
            part = slice(h * lanes, (h + 1) * lanes)
            for y in range(tgt_rows):
                rows = targets_ref[y, :, part].astype(jnp.float32)
                tall[pl.ds(y, tgt_width, stride=tgt_rows), :] = rows
            targets[:, part] = tall[...].astype(jnp.bfloat16)
        out_ref[...] = jnp.zeros_like(out_ref)

    def build(half, carry):
        row_no = step_no * pair_rows + half
        at = pl.ds(pl.multiple_of(half * lanes, lanes), lanes)
        center_y = jnp.broadcast_to(cents_ref[0, pl.ds(row_no, 1), :], tile)
        center_x = jnp.broadcast_to(cents_ref[1, pl.ds(row_no, 1), :], tile)
        ys = first_ref[0] + lax.broadcasted_iota(jnp.int32, tile, 0)
        zero = jnp.zeros(tile, jnp.float32)

        def spread(level):
            row_off = lax.shift_right_arithmetic(ys, level) - (
                lax.shift_right_arithmetic(center_y, level) - 4
            )
            hits = [row_off == a for a in range(9)]
            picked = []
            for b in range(9):
                acc = zero
                for a in range(9):
                    entry = wide[81 * level + 9 * a + b, pl.ds(row_no, 1), :]
                    acc = jnp.where(hits[a], jnp.broadcast_to(entry, tile), acc)
                picked.append(acc * (0.25**level) if level else acc)
            start = lax.shift_right_arithmetic(center_x, level) - 4
            turn = start & 15
            block = lax.shift_right_arithmetic(start, 4)
            slots = picked + [zero] * 7
            for bit in (8, 4, 2, 1):
                on = (turn & bit) != 0
                slots = [jnp.where(on, slots[(i - bit) % 16], slots[i]) for i in range(16)]
            homes = [jnp.where(turn > j, block + 1, block) for j in range(16)]
            return slots, homes

        offset = 0
        coarse = None
        for level in (3, 2, 1):
            slots, homes = spread(level)
            cells = tgt_width >> level
            for j in range(16):
                for q in range(cells // 16):
                    x = 16 * q + j
                    value = jnp.where(homes[j] == q, slots[j], 0.0)
                    if coarse is not None:
                        value = value + level_sums[coarse + (x >> 1)]
                    level_sums[offset + x] = value
            coarse = offset
            offset += cells
        slots, homes = spread(0)
        for j in range(0, 16, 2):
            for q in range(tgt_width // 16):
                x = 16 * q + j
                under = level_sums[coarse + (x >> 1)]
                left = jnp.where(homes[j] == q, slots[j], 0.0) + under
                right = jnp.where(homes[j + 1] == q, slots[j + 1], 0.0) + under
                pair = jnp.concatenate([left, right], axis=0).astype(jnp.bfloat16)
                corr_ref[x * tgt_rows : (x + 2) * tgt_rows, at] = pair
        return carry

    lax.fori_loop(0, pair_rows, build, 0)
    src = lax.dot_general(
        corr_ref[...],
        targets[...],
        (((0,), (0,)), ((), ())),
        preferred_element_type=jnp.float32,
    )
    exact = src * (1.0 / math.sqrt(width))
    src = exact.astype(jnp.bfloat16)
    rest = (exact - src.astype(jnp.float32)).astype(jnp.bfloat16)
    across = (((1,), (1,)), ((), ()))
    hidden = lax.dot_general(
        src, weight_ref[...], across, preferred_element_type=jnp.float32
    ) + lax.dot_general(rest, weight_ref[...], across, preferred_element_type=jnp.float32)
    hidden_ref[...] = hidden.astype(jnp.bfloat16)
    out_ref[...] += lax.dot_general(
        relu_ref[...], src, (((0,), (0,)), ((), ())), preferred_element_type=jnp.float32
    )


def source_pass(upstream, centers, relu_flat, target_feats, out_weight, row_first):
    src_rows, src_width, lookups = upstream.shape
    tgt_rows, tgt_width, width = target_feats.shape
    chans = relu_flat.shape[1]
    pair = 2 * src_width
    grads = jnp.transpose(upstream, (2, 0, 1))
    whole = lambda *shape: pl.BlockSpec(shape, lambda r, f: (0,) * len(shape))
    return pl.pallas_call(
        corr_kernel,
        out_shape=(
            jax.ShapeDtypeStruct((tgt_width * tgt_rows, src_rows * src_width), jnp.bfloat16),
            jax.ShapeDtypeStruct((src_rows * src_width, chans), jnp.bfloat16),
            jax.ShapeDtypeStruct((chans, width), jnp.float32),
        ),
        grid_spec=pltpu.PrefetchScalarGridSpec(
            num_scalar_prefetch=1,
            grid=(src_rows // 2,),
            in_specs=[
                whole(lookups, src_rows, src_width),
                whole(2, src_rows, src_width),
                whole(tgt_rows, tgt_width, width),
                pl.BlockSpec((pair, chans), lambda r, f: (r, 0)),
                whole(chans, width),
            ],
            out_specs=(
                pl.BlockSpec((tgt_width * tgt_rows, pair), lambda r, f: (0, r)),
                pl.BlockSpec((pair, chans), lambda r, f: (r, 0)),
                whole(chans, width),
            ),
            scratch_shapes=[
                pltpu.VMEM((lookups, src_rows, src_width), jnp.float32),
                pltpu.VMEM((tgt_width, tgt_rows, src_width), jnp.float32),
                pltpu.VMEM((tgt_width * tgt_rows, src_width), jnp.float32),
                pltpu.VMEM((tgt_width * tgt_rows, width), jnp.bfloat16),
            ],
        ),
        compiler_params=pltpu.CompilerParams(dimension_semantics=("arbitrary",)),
        cost_estimate=pl.CostEstimate(
            flops=4_000_000_000, bytes_accessed=7_000_000, transcendentals=0
        ),
        name="source_pass",
    )(row_first.reshape(1), grads, centers, target_feats, relu_flat, out_weight)


def target_kernel(core_ref, corr_ref, relu_ref, weight_ref, given_ref, kept_ref, feats):
    @pl.when(pl.program_id(0) == 0)
    def _():
        feats[...] = jnp.dot(
            relu_ref[...], weight_ref[...], preferred_element_type=jnp.float32
        ).astype(jnp.bfloat16)

    highs, _, both, sources = corr_ref.shape
    width = given_ref.shape[2]
    block = both // 2
    part = jnp.dot(
        corr_ref[...].reshape(highs * both, sources),
        feats[...],
        preferred_element_type=jnp.float32,
    )
    part = (part * (1.0 / math.sqrt(width))).astype(jnp.bfloat16).reshape(highs, 2, block, width)
    rows = highs * block
    first = core_ref[0] == 0

    @pl.when(first)
    def _():
        given_ref[0] = part[:, 1].reshape(rows, width)
        kept_ref[0] = part[:, 0].reshape(rows, width)

    @pl.when(jnp.logical_not(first))
    def _():
        given_ref[0] = part[:, 0].reshape(rows, width)
        kept_ref[0] = part[:, 1].reshape(rows, width)


def target_pass(corr, relu_flat, out_weight, core_at, highs, steps):
    cells, sources = corr.shape
    chans, width = out_weight.shape
    rows = cells // steps // 2
    whole = lambda *shape: pl.BlockSpec(shape, lambda r, f: (0,) * len(shape))
    part = pl.BlockSpec((1, rows, width), lambda r, f: (r, 0, 0))
    both = cells // steps // highs
    return pl.pallas_call(
        target_kernel,
        out_shape=(jax.ShapeDtypeStruct((steps, rows, width), jnp.bfloat16),) * 2,
        grid_spec=pltpu.PrefetchScalarGridSpec(
            num_scalar_prefetch=1,
            grid=(steps,),
            in_specs=[
                pl.BlockSpec((highs, 1, both, sources), lambda r, f: (0, r, 0, 0)),
                whole(sources, chans),
                whole(chans, width),
            ],
            out_specs=(part, part),
            scratch_shapes=[pltpu.VMEM((sources, width), jnp.bfloat16)],
        ),
        compiler_params=pltpu.CompilerParams(dimension_semantics=("arbitrary",)),
        cost_estimate=pl.CostEstimate(
            flops=2 * cells * sources * width, bytes_accessed=6_500_000, transcendentals=0
        ),
        name="target_pass",
    )(core_at.reshape(1), corr.reshape(highs, steps, both, sources), relu_flat, out_weight)


def shifted(wide):
    count = wide.shape[0]
    rows = lax.broadcasted_iota(jnp.int32, wide.shape, 0)
    left = jnp.where(rows == count - 1, 0.0, pltpu.roll(wide, count - 1, 0))
    right = jnp.where(rows == 0, 0.0, pltpu.roll(wide, 1, 0))
    return left, wide, right


def terms_kernel(at_ref, parts_ref, relu_ref, paired_ref, own_ref, linked_ref, out_ref, grad_ref, terms_ref):
    total = parts_ref[0].astype(jnp.float32)
    for k in range(1, parts_ref.shape[0]):
        total += parts_ref[k].astype(jnp.float32)
    grad = jnp.where(relu_ref[0].astype(jnp.float32) > 0, total, 0.0).astype(jnp.bfloat16)
    grad_ref[...] = grad
    near_grad = jnp.concatenate(shifted(grad.astype(jnp.float32)), axis=1).astype(jnp.bfloat16)
    even = at_ref[1] == 0
    before = jnp.where(even, linked_ref[...], paired_ref[...])
    after = jnp.where(even, paired_ref[...], linked_ref[...])
    near_input = jnp.concatenate([before, own_ref[...], after], axis=1)
    conv = lax.dot_general(
        near_input, near_grad, (((0,), (0,)), ((), ())), preferred_element_type=jnp.float32
    )
    near, _, across = terms_ref.shape
    conv = conv.reshape(near, conv.shape[0] // near, across)
    terms_ref[...] = jnp.concatenate([conv, out_ref[...]], axis=1).astype(jnp.bfloat16)


def weight_terms(parts, post_relu, inputs, out_term, tgt_at, odd, near):
    count, src_width, chans = parts.shape
    whole = lambda *shape: pl.BlockSpec(shape, lambda r, f: (0,) * len(shape))
    across = 3 * chans
    down = (across + chans) // near
    return pl.pallas_call(
        terms_kernel,
        out_shape=(
            jax.ShapeDtypeStruct((src_width, chans), jnp.bfloat16),
            jax.ShapeDtypeStruct((near, down, across), jnp.bfloat16),
        ),
        grid_spec=pltpu.PrefetchScalarGridSpec(
            num_scalar_prefetch=1,
            grid=(1,),
            in_specs=[
                whole(count, src_width, chans),
                pl.BlockSpec((1, src_width, chans), lambda r, f: (f[0], 0, 0)),
                whole(src_width, chans),
                whole(src_width, chans),
                whole(src_width, chans),
                whole(*out_term.shape),
            ],
            out_specs=(whole(src_width, chans), whole(near, down, across)),
        ),
        compiler_params=pltpu.CompilerParams(vmem_limit_bytes=8 * 2**20),
        name="weight_terms",
    )(jnp.stack([tgt_at, odd]), parts, post_relu, *inputs, out_term)


def near_sum_kernel(parts_ref, both_ref, joint_ref):
    total = parts_ref[0].astype(jnp.float32)
    for k in range(1, parts_ref.shape[0]):
        total += parts_ref[k].astype(jnp.float32)
    rows = total.shape[0]
    width = joint_ref.shape[2]
    last = total[:, width:]
    total = jnp.concatenate(
        [total[:, :width], jnp.concatenate([last[: rows // 2], last[rows // 2 :]], axis=1)], axis=0
    ).astype(jnp.bfloat16)
    block = both_ref.shape[1]
    for k in range(joint_ref.shape[0]):
        joint_ref[k, :block] = both_ref[k]
        joint_ref[k, block:] = total


def near_sum(parts, both):
    count, block, width = both.shape
    return pl.pallas_call(
        near_sum_kernel,
        out_shape=jax.ShapeDtypeStruct(
            (count, block + parts.shape[1] * parts.shape[2] // width, width), jnp.bfloat16
        ),
        compiler_params=pltpu.CompilerParams(vmem_limit_bytes=8 * 2**20),
        name="near_sum",
    )(parts, both)


def x_sum_kernel(parts_ref, joint_ref):
    total = parts_ref[0].astype(jnp.float32)
    for k in range(1, parts_ref.shape[0]):
        total += parts_ref[k].astype(jnp.float32)
    total = total.astype(jnp.bfloat16)
    count, rows, _ = joint_ref.shape
    piece = (count * rows - total.shape[0]) // (count - 1)
    block = rows - piece
    for k in range(count):
        joint_ref[k, :block] = total[k * block : (k + 1) * block]
        joint_ref[k, block:] = total[count * block :]


def x_sum(parts, count, block):
    _, rows, width = parts.shape
    return pl.pallas_call(
        x_sum_kernel,
        out_shape=jax.ShapeDtypeStruct(
            (count, block + rows - count * block, width), jnp.bfloat16
        ),
        compiler_params=pltpu.CompilerParams(vmem_limit_bytes=8 * 2**20),
        name="x_sum",
    )(parts)


def act_kernel(at_ref, grad_ref, paired_ref, linked_ref, weight_ref, act_ref):
    even = at_ref[0] == 0
    before = jnp.where(even, linked_ref[...], paired_ref[...])
    after = jnp.where(even, paired_ref[...], linked_ref[...])
    total = jnp.zeros(grad_ref.shape, jnp.float32)
    for p, row in enumerate((after, grad_ref[...], before)):
        for q, tap in enumerate(shifted(row.astype(jnp.float32))):
            total += lax.dot_general(
                tap.astype(jnp.bfloat16),
                weight_ref[p, q],
                (((1,), (1,)), ((), ())),
                preferred_element_type=jnp.float32,
            )
    act_ref[0] = total.astype(jnp.bfloat16)


def act_rows(block_grad, paired, linked, conv_weight, odd):
    whole = lambda *shape: pl.BlockSpec(shape, lambda r, f: (0,) * len(shape))
    cols, chans = block_grad.shape
    row = whole(cols, chans)
    return pl.pallas_call(
        act_kernel,
        out_shape=jax.ShapeDtypeStruct((1, cols, chans), jnp.bfloat16),
        grid_spec=pltpu.PrefetchScalarGridSpec(
            num_scalar_prefetch=1,
            grid=(1,),
            in_specs=[row, row, row, whole(3, 3, chans, chans)],
            out_specs=whole(1, cols, chans),
        ),
        compiler_params=pltpu.CompilerParams(vmem_limit_bytes=8 * 2**20),
        name="act_rows",
    )(odd.reshape(1), block_grad, paired, linked, conv_weight)


def far_sum_kernel(scale, parts_ref, tgt_ref, shared_ref, left, right):
    total = parts_ref[0].astype(jnp.float32)
    for k in range(1, parts_ref.shape[0]):
        total += parts_ref[k].astype(jnp.float32)
    tgt_rows, cols, width = tgt_ref.shape
    block = tgt_rows * cols
    near, rows, _ = shared_ref.shape
    left[...] = total[:block, : width // 2]
    right[...] = total[:block, width // 2 :]
    for y in range(tgt_rows):
        at = pl.ds(y, cols, stride=tgt_rows)
        row = jnp.concatenate([left[at, :], right[at, :]], axis=1)
        tgt_ref[y] = row.astype(jnp.bfloat16)
    first = total[block : block + rows]
    second = total[block + rows :]
    second = jnp.concatenate([second[:, : width // 2], second[:, width // 2 :]], axis=0)
    piece = (jnp.concatenate([first, second], axis=1) * scale).astype(jnp.bfloat16)
    for k in range(near):
        shared_ref[k] = piece


def far_sum(parts, tgt_rows, cols, near, rows, across, scale):
    width = parts.shape[2]
    return pl.pallas_call(
        functools.partial(far_sum_kernel, scale),
        out_shape=(
            jax.ShapeDtypeStruct((tgt_rows, cols, width), jnp.bfloat16),
            jax.ShapeDtypeStruct((near, rows, across), jnp.bfloat16),
        ),
        scratch_shapes=[pltpu.VMEM((tgt_rows * cols, width // 2), jnp.float32)] * 2,
        compiler_params=pltpu.CompilerParams(vmem_limit_bytes=8 * 2**20),
        name="far_sum",
    )(parts)


def unpack_kernel(totals_ref, conv_ref, out_ref):
    totals = totals_ref[...].astype(jnp.float32)
    near, _, across = totals.shape
    chans, width = out_ref.shape
    depth = across // near
    conv = totals[:, :depth, :].reshape(across, across)
    for p in range(3):
        for q in range(3):
            conv_ref[p, q] = conv[p * chans : (p + 1) * chans, q * chans : (q + 1) * chans]
    out_ref[...] = totals[:, depth:, :width].reshape(chans, width)


def unpack(totals, chans, width):
    return pl.pallas_call(
        unpack_kernel,
        out_shape=(
            jax.ShapeDtypeStruct((3, 3, chans, chans), jnp.float32),
            jax.ShapeDtypeStruct((chans, width), jnp.float32),
        ),
        compiler_params=pltpu.CompilerParams(vmem_limit_bytes=8 * 2**20),
        name="unpack",
    )(totals)


def body(upstream, centers, post_relu, conv_input, target_feats, out_weight, conv_weight):
    src_rows, src_width, _ = upstream.shape
    tgt_rows, tgt_width, width = target_feats.shape
    chans = post_relu.shape[2]
    src_devices = lax.axis_size(SRC)
    row_total = src_devices * src_rows
    near, highs, lows = lax.axis_size(NEAR), lax.axis_size("zh"), lax.axis_size("x")
    tgt_at = lax.axis_index(TGT)
    core_at = lax.axis_index("c")
    odd = lax.axis_index("zl")

    pairs = [(i, i ^ 1) for i in range(row_total)]
    links = [(i, i + 1) for i in range(1, row_total - 1, 2)]
    links += [(j, i) for i, j in links]
    own_input = conv_input[0]
    input_paired = lax.ppermute(own_input, ALL, pairs)
    input_linked = lax.ppermute(own_input, ALL, links)

    relu_flat = post_relu.reshape(src_rows * src_width, chans)
    corr, hidden, out_term = source_pass(
        upstream, centers, relu_flat, target_feats, out_weight, tgt_at * tgt_rows
    )
    hidden = lax.all_to_all(hidden.reshape(src_rows, src_width, chans), TGT, 0, 0)

    out_term = jnp.pad(
        out_term.reshape(near, chans // near, width), ((0, 0), (0, 0), (0, 3 * chans - width))
    )
    given, kept = target_pass(corr, relu_flat, out_weight, core_at, highs, lows)
    taken = lax.ppermute(given, "c", [(0, 1), (1, 0)])
    both = (kept.astype(jnp.float32) + taken.astype(jnp.float32)).astype(jnp.bfloat16)

    block_grad, terms = weight_terms(
        hidden, post_relu, (input_paired, own_input, input_linked), out_term, tgt_at, odd, near
    )
    terms = lax.all_to_all(terms, NEAR, 0, 0)
    grad_paired = lax.ppermute(block_grad, ALL, pairs)
    grad_linked = lax.ppermute(block_grad, ALL, links)
    joint = near_sum(terms, both)
    joint = lax.all_to_all(joint, "x", 0, 0)
    cols = tgt_width // src_devices
    joint = x_sum(joint, highs, cols * tgt_rows)
    joint = lax.all_to_all(joint, "zh", 0, 0)
    tgt_grad, pieces = far_sum(
        joint, tgt_rows, cols, near, terms.shape[1], terms.shape[2], 1.0 / row_total
    )
    pieces = lax.all_to_all(pieces, NEAR, 0, 0)
    act_grad = act_rows(block_grad, grad_paired, grad_linked, conv_weight, odd)
    conv_total, out_total = unpack(pieces, chans, width)
    return (tgt_grad, act_grad, out_total, conv_total)


def solution(mesh):
    grid = Mesh(mesh.devices.reshape(4, 4, 2, 4, 2), ALL)
    placed = (
        P(SRC, None, None),
        P(None, SRC, None),
        P(SRC, None, None),
        P(ALL, None, None),
        P(TGT, None, None),
        P(),
        P(),
    )
    return jax.shard_map(
        body,
        mesh=grid,
        in_specs=placed,
        out_specs=(P(TGT, SRC, None), P(ALL, None, None), P(), P()),
        check_vma=False,
    )
```

```python
import functools
import math

import jax
import jax.numpy as jnp
from jax import lax
from jax.experimental import pallas as pl
from jax.experimental.pallas import tpu as pltpu
from jax.sharding import Mesh, PartitionSpec as P


SRC = ("zh", "x", "c")
TGT = ("y", "zl")
ALL = SRC + TGT
NEAR = ("c", "y", "zl")


def source_kernel(
    highs,
    at_ref,
    grads_ref,
    cents_ref,
    targets_ref,
    relu_ref,
    weight_ref,
    hidden_ref,
    out_ref,
    given_ref,
    kept_ref,
    wide,
    level_sums,
    tall,
    targets,
    feats,
    sums,
    corr_a,
    corr_b,
):
    tgt_rows, tgt_width, width = targets_ref.shape
    src_rows, lanes = grads_ref.shape[1:]
    pair = 2 * lanes
    tile = (tgt_rows, lanes)
    f32, bf16 = jnp.float32, jnp.bfloat16
    scale = 1.0 / math.sqrt(width)
    across = (((1,), (1,)), ((), ()))
    down = (((0,), (0,)), ((), ()))

    wide[...] = grads_ref[...].astype(f32)
    for h in range(width // lanes):
        part = slice(h * lanes, (h + 1) * lanes)
        for y in range(tgt_rows):
            tall[pl.ds(y, tgt_width, stride=tgt_rows), :] = targets_ref[y, :, part].astype(f32)
        targets[:, part] = tall[...].astype(bf16)
    feats[...] = jnp.dot(relu_ref[...], weight_ref[...], preferred_element_type=f32).astype(bf16)

    def build(row_no, corr, at):
        center_y = jnp.broadcast_to(cents_ref[0, row_no : row_no + 1, :], tile)
        center_x = jnp.broadcast_to(cents_ref[1, row_no : row_no + 1, :], tile)
        ys = at_ref[0] + lax.broadcasted_iota(jnp.int32, tile, 0)
        zero = jnp.zeros(tile, f32)

        def spread(level):
            row_off = lax.shift_right_arithmetic(ys, level) - (
                lax.shift_right_arithmetic(center_y, level) - 4
            )
            hits = [row_off == a for a in range(9)]
            picked = []
            for b in range(9):
                acc = zero
                for a in range(9):
                    entry = wide[81 * level + 9 * a + b, row_no : row_no + 1, :]
                    acc = jnp.where(hits[a], jnp.broadcast_to(entry, tile), acc)
                picked.append(acc * (0.25**level) if level else acc)
            start = lax.shift_right_arithmetic(center_x, level) - 4
            turn = start & 15
            block = lax.shift_right_arithmetic(start, 4)
            slots = picked + [zero] * 7
            for bit in (8, 4, 2, 1):
                on = (turn & bit) != 0
                slots = [jnp.where(on, slots[(i - bit) % 16], slots[i]) for i in range(16)]
            homes = [jnp.where(turn > j, block + 1, block) for j in range(16)]
            return slots, homes

        offset = 0
        coarse = None
        for level in (3, 2, 1):
            slots, homes = spread(level)
            cells = tgt_width >> level
            for j in range(16):
                for q in range(cells // 16):
                    x = 16 * q + j
                    value = jnp.where(homes[j] == q, slots[j], 0.0)
                    if coarse is not None:
                        value = value + level_sums[coarse + (x >> 1)]
                    level_sums[offset + x] = value
            coarse = offset
            offset += cells
        slots, homes = spread(0)
        for j in range(0, 16, 2):
            for q in range(tgt_width // 16):
                x = 16 * q + j
                under = level_sums[coarse + (x >> 1)]
                left = jnp.where(homes[j] == q, slots[j], 0.0) + under
                right = jnp.where(homes[j + 1] == q, slots[j + 1], 0.0) + under
                both = jnp.concatenate([left, right], axis=0).astype(bf16)
                corr[x * tgt_rows : (x + 2) * tgt_rows, at : at + lanes] = both

    def products(step, corr):
        at = pl.ds(pl.multiple_of(step * pair, pair), pair)
        exact = lax.dot_general(corr[...], targets[...], down, preferred_element_type=f32) * scale
        src = exact.astype(bf16)
        rest = (exact - src.astype(f32)).astype(bf16)
        hidden = lax.dot_general(src, weight_ref[...], across, preferred_element_type=f32)
        hidden += lax.dot_general(rest, weight_ref[...], across, preferred_element_type=f32)
        hidden_ref[at, :] = hidden.astype(bf16)
        out = lax.dot_general(relu_ref[at, :], src, down, preferred_element_type=f32)
        part = jnp.dot(corr[...], feats[at, :], preferred_element_type=f32)
        return out, part

    steps = src_rows // 2
    ring = (corr_a, corr_b)
    for half in range(2):
        build(half, ring[0], half * lanes)
    for step in range(steps):
        out, part = products(step, ring[step % 2])
        if step == 0:
            out_ref[...] = out
            sums[...] = part
        else:
            out_ref[...] += out
            if step < steps - 1:
                sums[...] += part
        if step < steps - 1:
            for half in range(2):
                build(2 * step + 2 + half, ring[(step + 1) % 2], half * lanes)
    count, block, _ = given_ref.shape
    single = block // highs
    total = ((sums[...] + part) * scale).astype(bf16).reshape(highs, count, 2, single, width)
    first = at_ref[1] == 0

    @pl.when(first)
    def _():
        for k in range(count):
            given_ref[k] = total[:, k, 1].reshape(block, width)
            kept_ref[k] = total[:, k, 0].reshape(block, width)

    @pl.when(jnp.logical_not(first))
    def _():
        for k in range(count):
            given_ref[k] = total[:, k, 0].reshape(block, width)
            kept_ref[k] = total[:, k, 1].reshape(block, width)


def source_pass(upstream, centers, target_feats, relu_flat, out_weight, at, highs, lows):
    src_rows, src_width, lookups = upstream.shape
    tgt_rows, tgt_width, width = target_feats.shape
    chans = relu_flat.shape[1]
    sources, cells = src_rows * src_width, tgt_rows * tgt_width
    f32, bf16 = jnp.float32, jnp.bfloat16
    part = jax.ShapeDtypeStruct((lows, cells // lows // 2, width), bf16)
    return pl.pallas_call(
        functools.partial(source_kernel, highs),
        out_shape=(
            jax.ShapeDtypeStruct((sources, chans), bf16),
            jax.ShapeDtypeStruct((chans, width), f32),
            part,
            part,
        ),
        in_specs=[pl.BlockSpec(memory_space=pltpu.SMEM)] + [pl.BlockSpec(memory_space=pltpu.VMEM)] * 5,
        out_specs=[pl.BlockSpec(memory_space=pltpu.VMEM)] * 4,
        scratch_shapes=[
            pltpu.VMEM((lookups, src_rows, src_width), f32),
            pltpu.VMEM((tgt_width, tgt_rows, src_width), f32),
            pltpu.VMEM((cells, src_width), f32),
            pltpu.VMEM((cells, width), bf16),
            pltpu.VMEM((sources, width), bf16),
            pltpu.VMEM((cells, width), f32),
            pltpu.VMEM((cells, 2 * src_width), bf16),
            pltpu.VMEM((cells, 2 * src_width), bf16),
        ],
        cost_estimate=pl.CostEstimate(
            flops=4_000_000_000, bytes_accessed=4_000_000, transcendentals=0
        ),
        name="source_pass",
    )(at, jnp.transpose(upstream, (2, 0, 1)), centers, target_feats, relu_flat, out_weight)


def shifted(wide):
    count = wide.shape[0]
    rows = lax.broadcasted_iota(jnp.int32, wide.shape, 0)
    left = jnp.where(rows == count - 1, 0.0, pltpu.roll(wide, count - 1, 0))
    right = jnp.where(rows == 0, 0.0, pltpu.roll(wide, 1, 0))
    return left, wide, right


def terms_kernel(at_ref, parts_ref, relu_ref, paired_ref, own_ref, linked_ref, out_ref, grad_ref, terms_ref):
    total = parts_ref[0].astype(jnp.float32)
    for k in range(1, parts_ref.shape[0]):
        total += parts_ref[k].astype(jnp.float32)
    grad = jnp.where(relu_ref[0].astype(jnp.float32) > 0, total, 0.0).astype(jnp.bfloat16)
    grad_ref[...] = grad
    near_grad = jnp.concatenate(shifted(grad.astype(jnp.float32)), axis=1).astype(jnp.bfloat16)
    even = at_ref[1] == 0
    before = jnp.where(even, linked_ref[...], paired_ref[...])
    after = jnp.where(even, paired_ref[...], linked_ref[...])
    near_input = jnp.concatenate([before, own_ref[...], after], axis=1)
    conv = lax.dot_general(
        near_input, near_grad, (((0,), (0,)), ((), ())), preferred_element_type=jnp.float32
    )
    near, _, across = terms_ref.shape
    conv = conv.reshape(near, conv.shape[0] // near, across)
    terms_ref[...] = jnp.concatenate([conv, out_ref[...]], axis=1).astype(jnp.bfloat16)


def weight_terms(parts, post_relu, inputs, out_term, tgt_at, odd, near):
    count, src_width, chans = parts.shape
    whole = lambda *shape: pl.BlockSpec(shape, lambda r, f: (0,) * len(shape))
    across = 3 * chans
    down = (across + chans) // near
    return pl.pallas_call(
        terms_kernel,
        out_shape=(
            jax.ShapeDtypeStruct((src_width, chans), jnp.bfloat16),
            jax.ShapeDtypeStruct((near, down, across), jnp.bfloat16),
        ),
        grid_spec=pltpu.PrefetchScalarGridSpec(
            num_scalar_prefetch=1,
            grid=(1,),
            in_specs=[
                whole(count, src_width, chans),
                pl.BlockSpec((1, src_width, chans), lambda r, f: (f[0], 0, 0)),
                whole(src_width, chans),
                whole(src_width, chans),
                whole(src_width, chans),
                whole(*out_term.shape),
            ],
            out_specs=(whole(src_width, chans), whole(near, down, across)),
        ),
        compiler_params=pltpu.CompilerParams(vmem_limit_bytes=8 * 2**20),
        name="weight_terms",
    )(jnp.stack([tgt_at, odd]), parts, post_relu, *inputs, out_term)


def near_sum_kernel(parts_ref, both_ref, joint_ref):
    total = parts_ref[0].astype(jnp.float32)
    for k in range(1, parts_ref.shape[0]):
        total += parts_ref[k].astype(jnp.float32)
    rows = total.shape[0]
    width = joint_ref.shape[2]
    last = total[:, width:]
    total = jnp.concatenate(
        [total[:, :width], jnp.concatenate([last[: rows // 2], last[rows // 2 :]], axis=1)], axis=0
    ).astype(jnp.bfloat16)
    block = both_ref.shape[1]
    for k in range(joint_ref.shape[0]):
        joint_ref[k, :block] = both_ref[k]
        joint_ref[k, block:] = total


def near_sum(parts, both):
    count, block, width = both.shape
    return pl.pallas_call(
        near_sum_kernel,
        out_shape=jax.ShapeDtypeStruct(
            (count, block + parts.shape[1] * parts.shape[2] // width, width), jnp.bfloat16
        ),
        compiler_params=pltpu.CompilerParams(vmem_limit_bytes=8 * 2**20),
        name="near_sum",
    )(parts, both)


def x_sum_kernel(parts_ref, joint_ref):
    total = parts_ref[0].astype(jnp.float32)
    for k in range(1, parts_ref.shape[0]):
        total += parts_ref[k].astype(jnp.float32)
    total = total.astype(jnp.bfloat16)
    count, rows, _ = joint_ref.shape
    piece = (count * rows - total.shape[0]) // (count - 1)
    block = rows - piece
    for k in range(count):
        joint_ref[k, :block] = total[k * block : (k + 1) * block]
        joint_ref[k, block:] = total[count * block :]


def x_sum(parts, count, block):
    _, rows, width = parts.shape
    return pl.pallas_call(
        x_sum_kernel,
        out_shape=jax.ShapeDtypeStruct(
            (count, block + rows - count * block, width), jnp.bfloat16
        ),
        compiler_params=pltpu.CompilerParams(vmem_limit_bytes=8 * 2**20),
        name="x_sum",
    )(parts)


def act_kernel(at_ref, grad_ref, paired_ref, linked_ref, weight_ref, act_ref):
    even = at_ref[0] == 0
    before = jnp.where(even, linked_ref[...], paired_ref[...])
    after = jnp.where(even, paired_ref[...], linked_ref[...])
    total = jnp.zeros(grad_ref.shape, jnp.float32)
    for p, row in enumerate((after, grad_ref[...], before)):
        for q, tap in enumerate(shifted(row.astype(jnp.float32))):
            total += lax.dot_general(
                tap.astype(jnp.bfloat16),
                weight_ref[p, q],
                (((1,), (1,)), ((), ())),
                preferred_element_type=jnp.float32,
            )
    act_ref[0] = total.astype(jnp.bfloat16)


def act_rows(block_grad, paired, linked, conv_weight, odd):
    whole = lambda *shape: pl.BlockSpec(shape, lambda r, f: (0,) * len(shape))
    cols, chans = block_grad.shape
    row = whole(cols, chans)
    return pl.pallas_call(
        act_kernel,
        out_shape=jax.ShapeDtypeStruct((1, cols, chans), jnp.bfloat16),
        grid_spec=pltpu.PrefetchScalarGridSpec(
            num_scalar_prefetch=1,
            grid=(1,),
            in_specs=[row, row, row, whole(3, 3, chans, chans)],
            out_specs=whole(1, cols, chans),
        ),
        compiler_params=pltpu.CompilerParams(vmem_limit_bytes=8 * 2**20),
        name="act_rows",
    )(odd.reshape(1), block_grad, paired, linked, conv_weight)


def far_sum_kernel(scale, parts_ref, tgt_ref, shared_ref, left, right):
    total = parts_ref[0].astype(jnp.float32)
    for k in range(1, parts_ref.shape[0]):
        total += parts_ref[k].astype(jnp.float32)
    tgt_rows, cols, width = tgt_ref.shape
    block = tgt_rows * cols
    near, rows, _ = shared_ref.shape
    left[...] = total[:block, : width // 2]
    right[...] = total[:block, width // 2 :]
    for y in range(tgt_rows):
        at = pl.ds(y, cols, stride=tgt_rows)
        row = jnp.concatenate([left[at, :], right[at, :]], axis=1)
        tgt_ref[y] = row.astype(jnp.bfloat16)
    first = total[block : block + rows]
    second = total[block + rows :]
    second = jnp.concatenate([second[:, : width // 2], second[:, width // 2 :]], axis=0)
    piece = (jnp.concatenate([first, second], axis=1) * scale).astype(jnp.bfloat16)
    for k in range(near):
        shared_ref[k] = piece


def far_sum(parts, tgt_rows, cols, near, rows, across, scale):
    width = parts.shape[2]
    return pl.pallas_call(
        functools.partial(far_sum_kernel, scale),
        out_shape=(
            jax.ShapeDtypeStruct((tgt_rows, cols, width), jnp.bfloat16),
            jax.ShapeDtypeStruct((near, rows, across), jnp.bfloat16),
        ),
        scratch_shapes=[pltpu.VMEM((tgt_rows * cols, width // 2), jnp.float32)] * 2,
        compiler_params=pltpu.CompilerParams(vmem_limit_bytes=8 * 2**20),
        name="far_sum",
    )(parts)


def unpack_kernel(totals_ref, conv_ref, out_ref):
    totals = totals_ref[...].astype(jnp.float32)
    near, _, across = totals.shape
    chans, width = out_ref.shape
    depth = across // near
    conv = totals[:, :depth, :].reshape(across, across)
    for p in range(3):
        for q in range(3):
            conv_ref[p, q] = conv[p * chans : (p + 1) * chans, q * chans : (q + 1) * chans]
    out_ref[...] = totals[:, depth:, :width].reshape(chans, width)


def unpack(totals, chans, width):
    return pl.pallas_call(
        unpack_kernel,
        out_shape=(
            jax.ShapeDtypeStruct((3, 3, chans, chans), jnp.float32),
            jax.ShapeDtypeStruct((chans, width), jnp.float32),
        ),
        compiler_params=pltpu.CompilerParams(vmem_limit_bytes=8 * 2**20),
        name="unpack",
    )(totals)


def body(upstream, centers, post_relu, conv_input, target_feats, out_weight, conv_weight):
    src_rows, src_width, _ = upstream.shape
    tgt_rows, tgt_width, width = target_feats.shape
    chans = post_relu.shape[2]
    src_devices = lax.axis_size(SRC)
    row_total = src_devices * src_rows
    near, highs, lows = lax.axis_size(NEAR), lax.axis_size("zh"), lax.axis_size("x")
    tgt_at = lax.axis_index(TGT)
    core_at = lax.axis_index("c")
    odd = lax.axis_index("zl")

    pairs = [(i, i ^ 1) for i in range(row_total)]
    links = [(i, i + 1) for i in range(1, row_total - 1, 2)]
    links += [(j, i) for i, j in links]
    own_input = conv_input[0]
    input_paired = lax.ppermute(own_input, ALL, pairs)
    input_linked = lax.ppermute(own_input, ALL, links)

    relu_flat = post_relu.reshape(src_rows * src_width, chans)
    hidden, out_term, given, kept = source_pass(
        upstream,
        centers,
        target_feats,
        relu_flat,
        out_weight,
        jnp.stack([tgt_at * tgt_rows, core_at]),
        highs,
        lows,
    )
    hidden = lax.all_to_all(hidden.reshape(src_rows, src_width, chans), TGT, 0, 0)

    out_term = jnp.pad(
        out_term.reshape(near, chans // near, width), ((0, 0), (0, 0), (0, 3 * chans - width))
    )
    taken = lax.ppermute(given, "c", [(0, 1), (1, 0)])
    both = (kept.astype(jnp.float32) + taken.astype(jnp.float32)).astype(jnp.bfloat16)

    block_grad, terms = weight_terms(
        hidden, post_relu, (input_paired, own_input, input_linked), out_term, tgt_at, odd, near
    )
    terms = lax.all_to_all(terms, NEAR, 0, 0)
    grad_paired = lax.ppermute(block_grad, ALL, pairs)
    grad_linked = lax.ppermute(block_grad, ALL, links)
    joint = near_sum(terms, both)
    joint = lax.all_to_all(joint, "x", 0, 0)
    cols = tgt_width // src_devices
    joint = x_sum(joint, highs, cols * tgt_rows)
    joint = lax.all_to_all(joint, "zh", 0, 0)
    tgt_grad, pieces = far_sum(
        joint, tgt_rows, cols, near, terms.shape[1], terms.shape[2], 1.0 / row_total
    )
    pieces = lax.all_to_all(pieces, NEAR, 0, 0)
    act_grad = act_rows(block_grad, grad_paired, grad_linked, conv_weight, odd)
    conv_total, out_total = unpack(pieces, chans, width)
    return (tgt_grad, act_grad, out_total, conv_total)


def solution(mesh):
    grid = Mesh(mesh.devices.reshape(4, 4, 2, 4, 2), ALL)
    placed = (
        P(SRC, None, None),
        P(None, SRC, None),
        P(SRC, None, None),
        P(ALL, None, None),
        P(TGT, None, None),
        P(),
        P(),
    )
    return jax.shard_map(
        body,
        mesh=grid,
        in_specs=placed,
        out_specs=(P(TGT, SRC, None), P(ALL, None, None), P(), P()),
        check_vma=False,
    )
```

```python
import functools
import math

import jax
import jax.numpy as jnp
from jax import lax
from jax.experimental import pallas as pl
from jax.experimental.pallas import tpu as pltpu
from jax.sharding import Mesh, PartitionSpec as P


SRC = ("zh", "x", "c")
TGT = ("y", "zl")
ALL = SRC + TGT
NEAR = ("c", "y", "zl")


def source_kernel(
    highs,
    tgt_devices,
    at_ref,
    grads_ref,
    cents_ref,
    targets_ref,
    relu_ref,
    weight_ref,
    hidden_ref,
    out_ref,
    given_ref,
    kept_ref,
    wide,
    level_sums,
    tall,
    targets,
    feats,
    sums,
    corr_a,
    corr_b,
):
    tgt_rows, tgt_width, width = targets_ref.shape
    src_rows, lanes = grads_ref.shape[1:]
    pair = 2 * lanes
    tile = (tgt_rows, lanes)
    f32, bf16 = jnp.float32, jnp.bfloat16
    scale = 1.0 / math.sqrt(width)
    across = (((1,), (1,)), ((), ()))
    down = (((0,), (0,)), ((), ()))
    row_first = lax.rem(at_ref[0], tgt_devices) * tgt_rows

    wide[...] = grads_ref[...].astype(f32)
    for h in range(width // lanes):
        part = slice(h * lanes, (h + 1) * lanes)
        for y in range(tgt_rows):
            tall[pl.ds(y, tgt_width, stride=tgt_rows), :] = targets_ref[y, :, part].astype(f32)
        targets[:, part] = tall[...].astype(bf16)
    feats[...] = jnp.dot(relu_ref[...], weight_ref[...], preferred_element_type=f32).astype(bf16)

    def build(row_no, corr, at):
        center_y = jnp.broadcast_to(cents_ref[0, row_no : row_no + 1, :], tile)
        center_x = jnp.broadcast_to(cents_ref[1, row_no : row_no + 1, :], tile)
        ys = row_first + lax.broadcasted_iota(jnp.int32, tile, 0)
        zero = jnp.zeros(tile, f32)

        def spread(level):
            row_off = lax.shift_right_arithmetic(ys, level) - (
                lax.shift_right_arithmetic(center_y, level) - 4
            )
            hits = [row_off == a for a in range(9)]
            picked = []
            for b in range(9):
                acc = zero
                for a in range(9):
                    entry = wide[81 * level + 9 * a + b, row_no : row_no + 1, :]
                    acc = jnp.where(hits[a], jnp.broadcast_to(entry, tile), acc)
                picked.append(acc * (0.25**level) if level else acc)
            start = lax.shift_right_arithmetic(center_x, level) - 4
            turn = start & 15
            block = lax.shift_right_arithmetic(start, 4)
            slots = picked + [zero] * 7
            for bit in (8, 4, 2, 1):
                on = (turn & bit) != 0
                slots = [jnp.where(on, slots[(i - bit) % 16], slots[i]) for i in range(16)]
            homes = [jnp.where(turn > j, block + 1, block) for j in range(16)]
            return slots, homes

        offset = 0
        coarse = None
        for level in (3, 2, 1):
            slots, homes = spread(level)
            cells = tgt_width >> level
            for j in range(16):
                for q in range(cells // 16):
                    x = 16 * q + j
                    value = jnp.where(homes[j] == q, slots[j], 0.0)
                    if coarse is not None:
                        value = value + level_sums[coarse + (x >> 1)]
                    level_sums[offset + x] = value
            coarse = offset
            offset += cells
        slots, homes = spread(0)
        for j in range(0, 16, 2):
            for q in range(tgt_width // 16):
                x = 16 * q + j
                under = level_sums[coarse + (x >> 1)]
                left = jnp.where(homes[j] == q, slots[j], 0.0) + under
                right = jnp.where(homes[j + 1] == q, slots[j + 1], 0.0) + under
                both = jnp.concatenate([left, right], axis=0).astype(bf16)
                corr[x * tgt_rows : (x + 2) * tgt_rows, at : at + lanes] = both

    def products(step, corr):
        at = pl.ds(pl.multiple_of(step * pair, pair), pair)
        exact = lax.dot_general(corr[...], targets[...], down, preferred_element_type=f32) * scale
        src = exact.astype(bf16)
        rest = (exact - src.astype(f32)).astype(bf16)
        hidden = lax.dot_general(src, weight_ref[...], across, preferred_element_type=f32)
        hidden += lax.dot_general(rest, weight_ref[...], across, preferred_element_type=f32)
        hidden_ref[at, :] = hidden.astype(bf16)
        out = lax.dot_general(relu_ref[at, :], src, down, preferred_element_type=f32)
        part = jnp.dot(corr[...], feats[at, :], preferred_element_type=f32)
        return out, part

    steps = src_rows // 2
    ring = (corr_a, corr_b)
    for half in range(2):
        build(half, ring[0], half * lanes)
    for step in range(steps):
        out, part = products(step, ring[step % 2])
        if step == 0:
            out_ref[...] = out
            sums[...] = part
        else:
            out_ref[...] += out
            if step < steps - 1:
                sums[...] += part
        if step < steps - 1:
            for half in range(2):
                build(2 * step + 2 + half, ring[(step + 1) % 2], half * lanes)
    count, block, _ = given_ref.shape
    single = block // highs
    total = ((sums[...] + part) * scale).astype(bf16).reshape(highs, count, 2, single, width)
    first = lax.rem(lax.div(at_ref[0], tgt_devices), 2) == 0

    @pl.when(first)
    def _():
        for k in range(count):
            given_ref[k] = total[:, k, 1].reshape(block, width)
            kept_ref[k] = total[:, k, 0].reshape(block, width)

    @pl.when(jnp.logical_not(first))
    def _():
        for k in range(count):
            given_ref[k] = total[:, k, 0].reshape(block, width)
            kept_ref[k] = total[:, k, 1].reshape(block, width)


def source_pass(
    upstream, centers, target_feats, relu_flat, out_weight, at, highs, lows, tgt_devices
):
    src_rows, src_width, lookups = upstream.shape
    tgt_rows, tgt_width, width = target_feats.shape
    chans = relu_flat.shape[1]
    sources, cells = src_rows * src_width, tgt_rows * tgt_width
    f32, bf16 = jnp.float32, jnp.bfloat16
    part = jax.ShapeDtypeStruct((lows, cells // lows // 2, width), bf16)
    return pl.pallas_call(
        functools.partial(source_kernel, highs, tgt_devices),
        out_shape=(
            jax.ShapeDtypeStruct((sources, chans), bf16),
            jax.ShapeDtypeStruct((chans, width), f32),
            part,
            part,
        ),
        in_specs=[pl.BlockSpec(memory_space=pltpu.SMEM)] + [pl.BlockSpec(memory_space=pltpu.VMEM)] * 5,
        out_specs=[pl.BlockSpec(memory_space=pltpu.VMEM)] * 4,
        scratch_shapes=[
            pltpu.VMEM((lookups, src_rows, src_width), f32),
            pltpu.VMEM((tgt_width, tgt_rows, src_width), f32),
            pltpu.VMEM((cells, src_width), f32),
            pltpu.VMEM((cells, width), bf16),
            pltpu.VMEM((sources, width), bf16),
            pltpu.VMEM((cells, width), f32),
            pltpu.VMEM((cells, 2 * src_width), bf16),
            pltpu.VMEM((cells, 2 * src_width), bf16),
        ],
        cost_estimate=pl.CostEstimate(
            flops=4_000_000_000, bytes_accessed=4_000_000, transcendentals=0
        ),
        name="source_pass",
    )(at, jnp.transpose(upstream, (2, 0, 1)), centers, target_feats, relu_flat, out_weight)


def shifted(wide):
    count = wide.shape[0]
    rows = lax.broadcasted_iota(jnp.int32, wide.shape, 0)
    left = jnp.where(rows == count - 1, 0.0, pltpu.roll(wide, count - 1, 0))
    right = jnp.where(rows == 0, 0.0, pltpu.roll(wide, 1, 0))
    return left, wide, right


def neighbours(row_total, at_ref, paired_ref, linked_ref):
    row = at_ref[0]
    even = lax.rem(row, 2) == 0
    paired, linked = paired_ref[...], linked_ref[...]
    zero = jnp.zeros_like(paired)
    before = jnp.where(row == 0, zero, jnp.where(even, linked, paired))
    after = jnp.where(row == row_total - 1, zero, jnp.where(even, paired, linked))
    return before, after


def terms_kernel(row_total, at_ref, parts_ref, relu_ref, paired_ref, own_ref, linked_ref, out_ref, grad_ref, terms_ref):
    total = parts_ref[0].astype(jnp.float32)
    for k in range(1, parts_ref.shape[0]):
        total += parts_ref[k].astype(jnp.float32)
    grad = jnp.where(relu_ref[0].astype(jnp.float32) > 0, total, 0.0).astype(jnp.bfloat16)
    grad_ref[...] = grad
    near_grad = jnp.concatenate(shifted(grad.astype(jnp.float32)), axis=1).astype(jnp.bfloat16)
    before, after = neighbours(row_total, at_ref, paired_ref, linked_ref)
    near_input = jnp.concatenate([before, own_ref[...], after], axis=1)
    conv = lax.dot_general(
        near_input, near_grad, (((0,), (0,)), ((), ())), preferred_element_type=jnp.float32
    )
    near, _, across = terms_ref.shape
    conv = conv.reshape(near, conv.shape[0] // near, across)
    terms_ref[...] = jnp.concatenate([conv, out_ref[...]], axis=1).astype(jnp.bfloat16)


def weight_terms(parts, post_relu, inputs, out_term, row_at, row_total, near):
    count, src_width, chans = parts.shape
    whole = lambda *shape: pl.BlockSpec(shape, lambda r, f: (0,) * len(shape))
    across = 3 * chans
    down = (across + chans) // near
    return pl.pallas_call(
        functools.partial(terms_kernel, row_total),
        out_shape=(
            jax.ShapeDtypeStruct((src_width, chans), jnp.bfloat16),
            jax.ShapeDtypeStruct((near, down, across), jnp.bfloat16),
        ),
        grid_spec=pltpu.PrefetchScalarGridSpec(
            num_scalar_prefetch=1,
            grid=(1,),
            in_specs=[
                whole(count, src_width, chans),
                pl.BlockSpec((1, src_width, chans), lambda r, f: (lax.rem(f[0], count), 0, 0)),
                whole(src_width, chans),
                whole(src_width, chans),
                whole(src_width, chans),
                whole(*out_term.shape),
            ],
            out_specs=(whole(src_width, chans), whole(near, down, across)),
        ),
        compiler_params=pltpu.CompilerParams(vmem_limit_bytes=8 * 2**20),
        name="weight_terms",
    )(row_at, parts, post_relu, *inputs, out_term)


def near_sum_kernel(parts_ref, both_ref, joint_ref):
    total = parts_ref[0].astype(jnp.float32)
    for k in range(1, parts_ref.shape[0]):
        total += parts_ref[k].astype(jnp.float32)
    rows = total.shape[0]
    width = joint_ref.shape[2]
    last = total[:, width:]
    total = jnp.concatenate(
        [total[:, :width], jnp.concatenate([last[: rows // 2], last[rows // 2 :]], axis=1)], axis=0
    ).astype(jnp.bfloat16)
    block = both_ref.shape[1]
    for k in range(joint_ref.shape[0]):
        joint_ref[k, :block] = both_ref[k]
        joint_ref[k, block:] = total


def near_sum(parts, both):
    count, block, width = both.shape
    return pl.pallas_call(
        near_sum_kernel,
        out_shape=jax.ShapeDtypeStruct(
            (count, block + parts.shape[1] * parts.shape[2] // width, width), jnp.bfloat16
        ),
        compiler_params=pltpu.CompilerParams(vmem_limit_bytes=8 * 2**20),
        name="near_sum",
    )(parts, both)


def x_sum_kernel(parts_ref, joint_ref):
    total = parts_ref[0].astype(jnp.float32)
    for k in range(1, parts_ref.shape[0]):
        total += parts_ref[k].astype(jnp.float32)
    total = total.astype(jnp.bfloat16)
    count, rows, _ = joint_ref.shape
    piece = (count * rows - total.shape[0]) // (count - 1)
    block = rows - piece
    for k in range(count):
        joint_ref[k, :block] = total[k * block : (k + 1) * block]
        joint_ref[k, block:] = total[count * block :]


def x_sum(parts, count, block):
    _, rows, width = parts.shape
    return pl.pallas_call(
        x_sum_kernel,
        out_shape=jax.ShapeDtypeStruct(
            (count, block + rows - count * block, width), jnp.bfloat16
        ),
        compiler_params=pltpu.CompilerParams(vmem_limit_bytes=8 * 2**20),
        name="x_sum",
    )(parts)


def act_kernel(row_total, at_ref, grad_ref, paired_ref, linked_ref, weight_ref, act_ref):
    before, after = neighbours(row_total, at_ref, paired_ref, linked_ref)
    total = jnp.zeros(grad_ref.shape, jnp.float32)
    for p, row in enumerate((after, grad_ref[...], before)):
        for q, tap in enumerate(shifted(row.astype(jnp.float32))):
            total += lax.dot_general(
                tap.astype(jnp.bfloat16),
                weight_ref[p, q],
                (((1,), (1,)), ((), ())),
                preferred_element_type=jnp.float32,
            )
    act_ref[0] = total.astype(jnp.bfloat16)


def act_rows(block_grad, paired, linked, conv_weight, row_at, row_total):
    whole = lambda *shape: pl.BlockSpec(shape, lambda r, f: (0,) * len(shape))
    cols, chans = block_grad.shape
    row = whole(cols, chans)
    return pl.pallas_call(
        functools.partial(act_kernel, row_total),
        out_shape=jax.ShapeDtypeStruct((1, cols, chans), jnp.bfloat16),
        grid_spec=pltpu.PrefetchScalarGridSpec(
            num_scalar_prefetch=1,
            grid=(1,),
            in_specs=[row, row, row, whole(3, 3, chans, chans)],
            out_specs=whole(1, cols, chans),
        ),
        compiler_params=pltpu.CompilerParams(vmem_limit_bytes=8 * 2**20),
        name="act_rows",
    )(row_at, block_grad, paired, linked, conv_weight)


def far_sum_kernel(scale, parts_ref, tgt_ref, shared_ref, left, right):
    total = parts_ref[0].astype(jnp.float32)
    for k in range(1, parts_ref.shape[0]):
        total += parts_ref[k].astype(jnp.float32)
    tgt_rows, cols, width = tgt_ref.shape
    block = tgt_rows * cols
    near, rows, _ = shared_ref.shape
    left[...] = total[:block, : width // 2]
    right[...] = total[:block, width // 2 :]
    for y in range(tgt_rows):
        at = pl.ds(y, cols, stride=tgt_rows)
        row = jnp.concatenate([left[at, :], right[at, :]], axis=1)
        tgt_ref[y] = row.astype(jnp.bfloat16)
    first = total[block : block + rows]
    second = total[block + rows :]
    second = jnp.concatenate([second[:, : width // 2], second[:, width // 2 :]], axis=0)
    piece = (jnp.concatenate([first, second], axis=1) * scale).astype(jnp.bfloat16)
    for k in range(near):
        shared_ref[k] = piece


def far_sum(parts, tgt_rows, cols, near, rows, across, scale):
    width = parts.shape[2]
    return pl.pallas_call(
        functools.partial(far_sum_kernel, scale),
        out_shape=(
            jax.ShapeDtypeStruct((tgt_rows, cols, width), jnp.bfloat16),
            jax.ShapeDtypeStruct((near, rows, across), jnp.bfloat16),
        ),
        scratch_shapes=[pltpu.VMEM((tgt_rows * cols, width // 2), jnp.float32)] * 2,
        compiler_params=pltpu.CompilerParams(vmem_limit_bytes=8 * 2**20),
        name="far_sum",
    )(parts)


def unpack_kernel(totals_ref, conv_ref, out_ref):
    totals = totals_ref[...].astype(jnp.float32)
    near, _, across = totals.shape
    chans, width = out_ref.shape
    depth = across // near
    conv = totals[:, :depth, :].reshape(across, across)
    for p in range(3):
        for q in range(3):
            conv_ref[p, q] = conv[p * chans : (p + 1) * chans, q * chans : (q + 1) * chans]
    out_ref[...] = totals[:, depth:, :width].reshape(chans, width)


def unpack(totals, chans, width):
    return pl.pallas_call(
        unpack_kernel,
        out_shape=(
            jax.ShapeDtypeStruct((3, 3, chans, chans), jnp.float32),
            jax.ShapeDtypeStruct((chans, width), jnp.float32),
        ),
        compiler_params=pltpu.CompilerParams(vmem_limit_bytes=8 * 2**20),
        name="unpack",
    )(totals)


def body(upstream, centers, post_relu, conv_input, target_feats, out_weight, conv_weight):
    src_rows, src_width, _ = upstream.shape
    tgt_rows, tgt_width, width = target_feats.shape
    chans = post_relu.shape[2]
    src_devices, tgt_devices = lax.axis_size(SRC), lax.axis_size(TGT)
    row_total = src_devices * src_rows
    near, highs, lows = lax.axis_size(NEAR), lax.axis_size("zh"), lax.axis_size("x")
    row_at = lax.axis_index(ALL).reshape(1)

    pairs = [(i, i ^ 1) for i in range(row_total)]
    links = [(i, (i + 1) % row_total) for i in range(1, row_total, 2)]
    links += [(j, i) for i, j in links]
    own_input = conv_input[0]
    input_paired = lax.ppermute(own_input, ALL, pairs)
    input_linked = lax.ppermute(own_input, ALL, links)

    relu_flat = post_relu.reshape(src_rows * src_width, chans)
    hidden, out_term, given, kept = source_pass(
        upstream,
        centers,
        target_feats,
        relu_flat,
        out_weight,
        row_at,
        highs,
        lows,
        tgt_devices,
    )
    hidden = lax.all_to_all(hidden.reshape(src_rows, src_width, chans), TGT, 0, 0)

    out_term = jnp.pad(
        out_term.reshape(near, chans // near, width), ((0, 0), (0, 0), (0, 3 * chans - width))
    )
    taken = lax.ppermute(given, "c", [(0, 1), (1, 0)])
    both = (kept.astype(jnp.float32) + taken.astype(jnp.float32)).astype(jnp.bfloat16)

    block_grad, terms = weight_terms(
        hidden, post_relu, (input_paired, own_input, input_linked), out_term, row_at, row_total, near
    )
    terms = lax.all_to_all(terms, NEAR, 0, 0)
    grad_paired = lax.ppermute(block_grad, ALL, pairs)
    grad_linked = lax.ppermute(block_grad, ALL, links)
    joint = near_sum(terms, both)
    joint = lax.all_to_all(joint, "x", 0, 0)
    cols = tgt_width // src_devices
    joint = x_sum(joint, highs, cols * tgt_rows)
    joint = lax.all_to_all(joint, "zh", 0, 0)
    tgt_grad, pieces = far_sum(
        joint, tgt_rows, cols, near, terms.shape[1], terms.shape[2], 1.0 / row_total
    )
    pieces = lax.all_to_all(pieces, NEAR, 0, 0)
    act_grad = act_rows(
        block_grad, grad_paired, grad_linked, conv_weight, row_at, row_total
    )
    conv_total, out_total = unpack(pieces, chans, width)
    return (tgt_grad, act_grad, out_total, conv_total)


def solution(mesh):
    grid = Mesh(mesh.devices.reshape(4, 4, 2, 4, 2), ALL)
    placed = (
        P(SRC, None, None),
        P(None, SRC, None),
        P(SRC, None, None),
        P(ALL, None, None),
        P(TGT, None, None),
        P(),
        P(),
    )
    return jax.shard_map(
        body,
        mesh=grid,
        in_specs=placed,
        out_specs=(P(TGT, SRC, None), P(ALL, None, None), P(), P()),
        check_vma=False,
    )
```
